32 devices in a mesh: head: 4 (over y, x), space: 8 (over z, core).
Axes of the slice: x: 2, y: 2, z: 4, core: 2. Of those that a mesh axis runs over, the one named last changes fastest.
Arguments:
- features: bfloat16 [1024, 512, 256], P('space', 'head'), may hold values from -6 to 6
- stain_delta: float32 [256], replicated, may hold values from -0.4 to 0.4
- tissue: int32 [16, 8], P('space', 'head'), may hold values from 0 to 1, as said below
- reduce_weight: bfloat16 [256, 128], replicated, may hold values from -0.375 to 0.375
- spatial_weight: bfloat16 [3, 3, 128, 128], replicated, may hold values from -0.1875 to 0.1875
- expand_weight: bfloat16 [128, 512], replicated, may hold values from -0.5 to 0.5
- shortcut_weight: bfloat16 [256, 512], replicated, may hold values from -0.375 to 0.375
- attn_tanh: float32 [512, 256], replicated, may hold values from -1 to 1
- attn_sigm: float32 [512, 256], replicated, may hold values from -1 to 1
- attn_out: float32 [256], replicated, may hold values from -2 to 2
- classifier: float32 [512], replicated, may hold values from -0.75 to 0.75
- step_dir: int32 [256], replicated, may hold values from 0 to 1
Outputs:
- feature_grad: bfloat16 [1024, 512, 256], P('space', 'head')
- new_delta: float32 [256], replicated
The draws below stay inside these ranges and needn't reach their ends.
Inputs may be any that keep to these rules, and one draw needn't show every extreme that they name: The tile at the slide's first row and column holds tissue.
All inputs are finite; a program needn't handle non-finite values.
Results may differ from the reference program's by a relative error of at most 0.0065.
Values may be sent and summed in bfloat16 or wider, within the bound.
A program may use at most 128 MiB of HBM per device.

```python
import jax
import jax.numpy as jnp
from jax import lax

CIN = 256
MID = 128
COUT = 512
ATT = 256
TILE = 64
HGT = 1024
WID = 512
ALPHA = 1


def draw_tissue(key, part):
    marks = jax.random.randint(key, (HGT // TILE, WID // TILE), 0, 5)
    marks = jnp.where(marks >= 2, 1, 0).astype(jnp.int32)
    return marks.at[0, 0].set(1)


def gate_noise(key, salt):
    noise = jax.random.normal(jax.random.fold_in(key, salt), (COUT, ATT), jnp.float32)
    return jnp.clip(noise, -2.5, 2.5) * (8.0 / COUT) ** 0.5


def draw_attn_tanh(key, part):
    noise = gate_noise(key, 21)
    return noise


def draw_attn_sigm(key, part):
    noise = gate_noise(key, 22)
    return noise


def draw_attn_out(key, part):
    values = jnp.clip(jax.random.normal(jax.random.fold_in(key, 32), (ATT,), jnp.float32), -2.5, 2.5) * (16.0 / ATT) ** 0.5
    return values


def touch_ends(entries, key, low, top_value):
    spot = [jax.random.randint(jax.random.fold_in(key, axis), (), 0, length) for axis, length in enumerate(entries.shape)]
    widest = entries.shape.index(max(entries.shape))
    next_to = spot[:widest] + [(spot[widest] + 1) % entries.shape[widest]] + spot[widest + 1:]
    return entries.at[tuple(spot)].set(low).at[tuple(next_to)].set(top_value)


def level_of(own_key, extent, cuts, least, high):
    factor_of = 1.0
    for axis_at, parts in cuts:
        steps = jax.random.uniform(jax.random.fold_in(jax.random.fold_in(own_key, 6), axis_at), (parts,), jnp.float32, least / len(cuts), high / len(cuts))
        factor_of = factor_of * jnp.repeat(jnp.exp(steps), extent[axis_at] // parts).reshape((-1,) + (1,) * (len(extent) - 1 - axis_at))
    return factor_of


def scatter_about(own_key, dims, scale, most, split=(), held_as=jnp.bfloat16):
    loudness = level_of(own_key, dims, split, -0.22, 0.18) if split else 1.0
    entries = jax.random.normal(own_key, dims, jnp.float32) * scale * loudness
    return jnp.minimum(jnp.maximum(entries, -most), most).astype(held_as)


def setup_inputs(seed: int = 0) -> dict:
    splits = jax.random.split(jax.random.key(seed), 13)
    return {
        "features": scatter_about(splits[0], (HGT, WID, CIN), 1.0, 6.0, ((0, 8), (1, 4))),
        "stain_delta": jnp.clip(jax.random.uniform(splits[1], (CIN,), jnp.float32, -0.4, 0.4), -0.4, 0.4),
        "tissue": draw_tissue(jax.random.fold_in(splits[12], 71), 0),
        "reduce_weight": scatter_about(splits[3], (CIN, MID), CIN ** -0.5, 0.375),
        "spatial_weight": scatter_about(splits[4], (3, 3, MID, MID), (9 * MID) ** -0.5, 0.1875),
        "expand_weight": scatter_about(splits[5], (MID, COUT), MID ** -0.5, 0.5),
        "shortcut_weight": scatter_about(splits[6], (CIN, COUT), CIN ** -0.5, 0.375),
        "attn_tanh": draw_attn_tanh(jax.random.fold_in(splits[12], 71), 0),
        "attn_sigm": draw_attn_sigm(jax.random.fold_in(splits[12], 71), 0),
        "attn_out": draw_attn_out(jax.random.fold_in(splits[12], 71), 0),
        "classifier": scatter_about(splits[10], (COUT,), (COUT // 8) ** -0.5, 0.75, (), jnp.float32),
        "step_dir": touch_ends(jax.random.randint(splits[11], (CIN,), 0, 2), jax.random.fold_in(splits[11], 1), 0, 1).astype(jnp.int32),
    }


def silu_slope(value):
    sig = jax.nn.sigmoid(value)
    return sig * (1.0 + value * (1.0 - sig))

def reference(features, stain_delta, tissue, reduce_weight, spatial_weight, expand_weight, shortcut_weight, attn_tanh, attn_sigm, attn_out, classifier, step_dir):
    hp = lax.Precision.HIGHEST
    rows, cols, chan = features.shape
    mid = reduce_weight.shape[1]
    cout = expand_weight.shape[1]
    scale = 1.0 + stain_delta
    perturbed = (features.astype(jnp.float32) * scale).astype(jnp.bfloat16)
    reduce_pre = jnp.dot(perturbed.reshape(-1, chan), reduce_weight, preferred_element_type=jnp.float32).reshape(rows, cols, mid)
    reduced = jax.nn.silu(reduce_pre).astype(jnp.bfloat16)
    padded = jnp.pad(reduced, ((1, 0), (1, 0), (0, 0)))
    orow, ocol = (rows // 2, cols // 2)
    acc = jnp.zeros((orow * ocol, mid), jnp.float32)
    for a in range(3):
        for b in range(3):
            tap = padded[a:a + rows:2, b:b + cols:2].reshape(-1, mid)
            acc = acc + jnp.dot(tap, spatial_weight[a, b], preferred_element_type=jnp.float32)
    spatial = jax.nn.silu(acc).astype(jnp.bfloat16)
    short_in = perturbed[::2, ::2].reshape(-1, chan)
    preact = jnp.dot(spatial, expand_weight, preferred_element_type=jnp.float32) + jnp.dot(short_in, shortcut_weight, preferred_element_type=jnp.float32)
    block = jax.nn.silu(preact).reshape(orow, ocol, cout)
    half = TILE // 2
    embed = block.reshape(orow // half, half, ocol // half, half, cout).mean(axis=(1, 3))
    tiles_r, tiles_c = (embed.shape[0], embed.shape[1])
    flat = embed.reshape(-1, cout)
    tval = jnp.tanh(jnp.dot(flat, attn_tanh, precision=hp))
    gval = jax.nn.sigmoid(jnp.dot(flat, attn_sigm, precision=hp))
    score = jnp.dot(tval * gval, attn_out, precision=hp)
    live = tissue.reshape(-1) > 0
    top = jnp.max(jnp.where(live, score, -1e+30))
    weights = jnp.where(live, jnp.exp(score - top), 0.0)
    total = jnp.sum(weights)
    pooled = jnp.dot(weights, flat, precision=hp) / total
    prob = weights / total
    mean_logit = jnp.dot(pooled, classifier, precision=hp)
    dprob = jnp.dot(flat, classifier, precision=hp)
    dscore = prob * (dprob - mean_logit)
    datt = dscore[:, None] * attn_out[None, :]
    dtanh = datt * gval * (1.0 - tval * tval)
    dsigm = datt * tval * gval * (1.0 - gval)
    dembed = prob[:, None] * classifier[None, :] + jnp.dot(dtanh, attn_tanh.T, precision=hp) + jnp.dot(dsigm, attn_sigm.T, precision=hp)
    dembed = dembed.reshape(tiles_r, 1, tiles_c, 1, cout) / float(half * half)
    dblock = jnp.broadcast_to(dembed, (tiles_r, half, tiles_c, half, cout)).reshape(-1, cout)
    dpre = (dblock * silu_slope(preact)).astype(jnp.bfloat16)
    dspatial = (jnp.dot(dpre, expand_weight.T, preferred_element_type=jnp.float32) * silu_slope(acc)).astype(jnp.bfloat16)
    dshort = jnp.dot(dpre, shortcut_weight.T, preferred_element_type=jnp.float32).reshape(orow, ocol, chan)
    dpad = jnp.zeros((rows + 1, cols + 1, mid), jnp.float32)
    for a in range(3):
        for b in range(3):
            part = jnp.dot(dspatial, spatial_weight[a, b].T, preferred_element_type=jnp.float32).reshape(orow, ocol, mid)
            dpad = dpad.at[a:a + rows:2, b:b + cols:2].add(part)
    dreduced = (dpad[1:, 1:] * silu_slope(reduce_pre)).astype(jnp.bfloat16)
    dinput = jnp.dot(dreduced.reshape(-1, mid), reduce_weight.T, preferred_element_type=jnp.float32).reshape(rows, cols, chan)
    dinput = dinput.at[::2, ::2].add(dshort)
    feature_grad = (dinput * scale).astype(jnp.bfloat16)
    ddelta = lax.optimization_barrier(jnp.sum(dinput * features.astype(jnp.float32), axis=(0, 1)))
    norm_size = jnp.sqrt(jnp.mean(ddelta * ddelta) + 1e-06)
    direction = (2 * step_dir - 1).astype(jnp.float32)
    new_delta = stain_delta + direction * float(ALPHA) * ddelta / norm_size
    return (feature_grad, new_delta)
```

```python
import functools

import jax
import jax.numpy as jnp
from jax import lax
from jax.experimental import pallas as pl
from jax.experimental.pallas import tpu as pltpu
from jax.sharding import PartitionSpec as P

TILE = 64
ALPHA = 1
BLOCK = 16
SUB = 8
F32 = jnp.float32
BF16 = jnp.bfloat16
HP = lax.Precision.HIGHEST


def sigm(value):
    return 0.5 + 0.5 * jnp.tanh(0.5 * value)


def passed_along(value, axis, steps):
    count = lax.axis_size(axis)
    first, last = (max(0, -steps), min(count, count - steps))
    return lax.ppermute(value, axis, [(source, source + steps) for source in range(first, last)])


def dot(a, b):
    return jnp.dot(a, b, preferred_element_type=F32)


def forward_kernel(
    tiles_r, tiles_c, x_ref, up_ref, left_ref, wr_ref, wc_ref, wp_ref, at_ref, as_ref, ao_ref, live_ref,
    slope1_ref, slope2_ref, slope3_ref, pay_ref, embed_ref, tval_ref, gval_ref, score_ref,
    red, lo, hi, taps, sums,
):
    step = pl.program_id(0)
    rows, cols, chan = x_ref.shape
    mid = wr_ref.shape[1]
    cout = wp_ref.shape[1]
    orow, ocol = rows // 2, cols // 2
    half = TILE // 2

    def put_taps(slot, source):
        for b, start in enumerate((SUB - 1, SUB, SUB + 1)):
            taps[slot, :, b * mid : (b + 1) * mid] = source[pl.ds(start, ocol, stride=2), :].astype(BF16)

    @pl.when(step == 0)
    def _():
        put_taps(0, up_ref)
        sums[...] = jnp.zeros_like(sums)

    @pl.when(step > 0)
    def _():
        taps[0] = taps[rows]

    pre = dot(x_ref[...].reshape(rows * cols, chan), wr_ref[...])
    sig = sigm(pre)
    act = pre * sig
    slope1_ref[...] = (sig + act * (1.0 - sig)).reshape(rows, cols, mid).astype(BF16)
    red[:, SUB:, :] = act.reshape(rows, cols, mid)
    red[:, SUB - 1 : SUB, :] = left_ref[...]
    for r in range(rows):
        put_taps(r + 1, red.at[r])
    acc = jnp.zeros((orow * ocol, mid), F32)
    for a in range(3):
        part = jnp.stack([taps[2 * i + a] for i in range(orow)], axis=0)
        acc = acc + dot(part.reshape(orow * ocol, 3 * mid), wc_ref[a])
    sig = sigm(acc)
    act = acc * sig
    slope2_ref[...] = (sig + act * (1.0 - sig)).reshape(orow, ocol, mid).astype(BF16)
    short = []
    for i in range(orow):
        lo[i] = x_ref[2 * i, :, : chan // 2].astype(F32)
        hi[i] = x_ref[2 * i, :, chan // 2 :].astype(F32)
    for i in range(orow):
        short.append(
            jnp.concatenate(
                [lo.at[i][pl.ds(0, ocol, stride=2), :].astype(BF16), hi.at[i][pl.ds(0, ocol, stride=2), :].astype(BF16)],
                axis=1,
            )
        )
    short = jnp.stack(short, axis=0).reshape(orow * ocol, chan)
    preact = dot(jnp.concatenate([act.astype(BF16), short], axis=1), wp_ref[...])
    sig = sigm(preact)
    act = preact * sig
    slope3_ref[...] = (sig + act * (1.0 - sig)).reshape(orow, ocol, cout).astype(BF16)
    cells = jnp.sum(act.reshape(orow, tiles_c, half // SUB, SUB, cout), axis=(0, 2))
    trow = (step * orow) // half
    for c in range(tiles_c):
        slot = trow * tiles_c + c
        sums[slot] = sums[slot] + cells[c]

    @pl.when(step == pl.num_programs(0) - 1)
    def _():
        embed = jnp.sum(sums[...], axis=1) * (1.0 / (half * half))
        tval = jnp.tanh(jnp.dot(embed, at_ref[...], precision=HP, preferred_element_type=F32))
        gval = sigm(jnp.dot(embed, as_ref[...], precision=HP, preferred_element_type=F32))
        score = jnp.sum(tval * gval * ao_ref[...], axis=1, keepdims=True)
        live = live_ref[:, 0:1] > 0
        top = jnp.max(jnp.where(live, score, -1e30), axis=0, keepdims=True)
        weight = jnp.where(live, jnp.exp(score - top), 0.0)
        pay_ref[0:1, :] = jnp.sum(weight * embed, axis=0, keepdims=True)
        pay_ref[1:2, :] = jnp.broadcast_to(jnp.sum(weight, axis=0, keepdims=True), (1, cout))
        pay_ref[2:3, :] = jnp.broadcast_to(top, (1, cout))
        pay_ref[3:8, :] = jnp.zeros((5, cout), F32)
        embed_ref[...] = embed
        tval_ref[...] = tval
        gval_ref[...] = gval
        score_ref[...] = jnp.broadcast_to(score, score_ref.shape)


def exchange_kernel(sizes, softmax, pay_ref, out_ref, got0, got1, mine, send0, send1, recv0, recv1):
    axes = ("head", "space")
    place = tuple(lax.axis_index(axis) for axis in axes)
    gots, sends, recvs = (got0, got1), (send0, send1), (recv0, recv1)

    def peer(k, hop):
        other = lax.rem(place[k] + hop, sizes[k])
        return (other, place[1]) if k == 0 else (place[0], other)

    barrier = pltpu.get_barrier_semaphore()
    for k in range(2):
        @pl.loop(1, sizes[k])
        def _(hop):
            pl.semaphore_signal(barrier, inc=1, device_id=peer(k, hop), device_id_type=pl.DeviceIdType.MESH)
    pl.semaphore_wait(barrier, sizes[0] + sizes[1] - 2)

    mine[0] = pay_ref[...]
    for k in range(2):
        got, n = gots[k], sizes[k]

        def copy(hop):
            return pltpu.make_async_remote_copy(
                src_ref=mine.at[k],
                dst_ref=got.at[hop],
                send_sem=sends[k].at[hop],
                recv_sem=recvs[k].at[hop],
                device_id=peer(k, hop),
                device_id_type=pl.DeviceIdType.MESH,
            )

        @pl.loop(1, n)
        def _(hop):
            copy(hop).start()

        got[0] = mine[k]

        @pl.loop(1, n)
        def _(hop):
            copy(hop).wait()

        every = got[...]
        if softmax:
            top = jnp.max(every[:, 2:3, :], axis=0)
            factor = jnp.exp(every[:, 2:3, :] - top[None])
            total = jnp.sum(every[:, 0:2, :] * factor, axis=0)
            result = jnp.concatenate([total, top, jnp.zeros((5, top.shape[1]), F32)], axis=0)
        else:
            result = jnp.sum(every, axis=0)
        if k == 0:
            mine[1] = result
        else:
            out_ref[...] = result


def exchange(payload, softmax, ident):
    sizes = (lax.axis_size("head"), lax.axis_size("space"))
    return pl.pallas_call(
        functools.partial(exchange_kernel, sizes, softmax),
        out_shape=jax.ShapeDtypeStruct(payload.shape, F32),
        in_specs=[pl.BlockSpec(memory_space=pltpu.VMEM)],
        out_specs=pl.BlockSpec(memory_space=pltpu.VMEM),
        scratch_shapes=[
            pltpu.VMEM((sizes[0],) + payload.shape, F32),
            pltpu.VMEM((sizes[1],) + payload.shape, F32),
            pltpu.VMEM((2,) + payload.shape, F32),
            pltpu.SemaphoreType.DMA((sizes[0],)),
            pltpu.SemaphoreType.DMA((sizes[1],)),
            pltpu.SemaphoreType.DMA((sizes[0],)),
            pltpu.SemaphoreType.DMA((sizes[1],)),
        ],
        compiler_params=pltpu.CompilerParams(collective_id=ident, has_side_effects=True),
        name="exchange_softmax" if softmax else "exchange_sum",
    )(payload)


def spread(dembed_ref, first, tiles_c, half):
    cout = dembed_ref.shape[1]
    return jnp.concatenate(
        [jnp.broadcast_to(dembed_ref[pl.ds(first + c, 1), :], (half, cout)) for c in range(tiles_c)], axis=0
    )


def edge_kernel(
    tiles_r, tiles_c, comb_ref, embed_ref, tval_ref, gval_ref, score_ref, live_ref, ao_ref, cls_ref, at_ref, as_ref,
    we_ref, row3_ref, row2_ref, col3_ref, col2_ref, dembed_ref, drow_ref, dcol_ref,
):
    half = TILE // 2
    embed, tval, gval = embed_ref[...], tval_ref[...], gval_ref[...]
    ao, cls = ao_ref[...], cls_ref[...]
    pooled = comb_ref[0:1, :] / comb_ref[1:2, :]
    total, top = comb_ref[1:2, 0:1], comb_ref[2:3, 0:1]
    live = live_ref[:, 0:1] > 0
    prob = jnp.where(live, jnp.exp(score_ref[:, 0:1] - top), 0.0) / total
    gap = jnp.sum(embed * cls, axis=1, keepdims=True) - jnp.sum(pooled * cls, axis=1, keepdims=True)
    datt = (prob * gap) * ao
    dtanh = datt * gval * (1.0 - tval * tval)
    dsigm = datt * tval * gval * (1.0 - gval)
    back = (((1,), (1,)), ((), ()))
    dembed = (
        prob * cls
        + lax.dot_general(dtanh, at_ref[...], back, precision=HP, preferred_element_type=F32)
        + lax.dot_general(dsigm, as_ref[...], back, precision=HP, preferred_element_type=F32)
    )
    dembed_ref[...] = dembed * (1.0 / (half * half))
    dpre = (row3_ref[0].astype(F32) * spread(dembed_ref, 0, tiles_c, half)).astype(BF16)
    drow_ref[...] = (dot(dpre, we_ref[...]) * row2_ref[0].astype(F32)).astype(BF16)
    cout = embed.shape[1]
    down = jnp.concatenate(
        [jnp.broadcast_to(dembed_ref[r * tiles_c : r * tiles_c + 1, :], (half, cout)) for r in range(tiles_r)], axis=0
    )
    dpre = (col3_ref[...].astype(F32) * down).astype(BF16)
    dcol_ref[...] = (dot(dpre, we_ref[...]) * col2_ref[...].astype(F32)).astype(BF16)


def backward_kernel(
    tiles_c, x_ref, slope1_ref, slope2_ref, slope3_ref, dembed_ref, right_ref, low_ref, wb_ref, wt_ref, wo_ref,
    out_ref, grad_ref, dsx, drs, slo, shi,
):
    step = pl.program_id(0)
    rows, cols, chan = x_ref.shape
    orow, ocol, mid = slope2_ref.shape
    cout = slope3_ref.shape[2]
    half = TILE // 2
    block = pl.num_programs(0) - 1 - step
    trow = (block * orow) // half

    @pl.when(step == 0)
    def _():
        dsx[orow] = low_ref[...]
        slo[...] = jnp.zeros_like(slo)
        shi[...] = jnp.zeros_like(shi)
        grad_ref[...] = jnp.zeros_like(grad_ref)

    @pl.when(step > 0)
    def _():
        dsx[orow] = dsx[0]

    dpre = (slope3_ref[...].astype(F32) * spread(dembed_ref, trow * tiles_c, tiles_c, half)[None]).astype(BF16)
    both = dot(dpre.reshape(orow * ocol, cout), wb_ref[...])
    dsx[0:orow, 0:ocol, :] = both[:, :mid].reshape(orow, ocol, mid) * slope2_ref[...].astype(F32)
    dsx[0:orow, ocol : ocol + 1, :] = right_ref[...]
    for i in range(orow):
        slo[i, pl.ds(0, ocol, stride=2), :] = both[i * ocol : (i + 1) * ocol, mid : mid + chan // 2]
        shi[i, pl.ds(0, ocol, stride=2), :] = both[i * ocol : (i + 1) * ocol, mid + chan // 2 :]
    four = jnp.concatenate(
        [
            dsx[di : di + orow, dj : dj + ocol, :].astype(BF16).reshape(orow * ocol, mid)
            for di in range(2)
            for dj in range(2)
        ],
        axis=1,
    )
    grads = dot(four, wt_ref[...])
    for i in range(orow):
        for di in range(2):
            for dj in range(2):
                n = 2 * di + dj
                drs[2 * i + di, pl.ds(dj, ocol, stride=2), :] = grads[i * ocol : (i + 1) * ocol, n * mid : (n + 1) * mid]
    dred = (drs[...] * slope1_ref[...].astype(F32)).astype(BF16)
    dinput = dot(dred.reshape(rows * cols, mid), wo_ref[...]).reshape(rows, cols, chan)
    total = jnp.zeros((SUB, chan), F32)
    for r in range(rows):
        value = dinput[r]
        if r % 2 == 0:
            value = value + jnp.concatenate([slo[r // 2], shi[r // 2]], axis=1)
        out_ref[r] = value.astype(BF16)
        total = total + jnp.sum((value * x_ref[r].astype(F32)).reshape(cols // SUB, SUB, chan), axis=0)
    grad_ref[...] += total


def whole(shape):
    return pl.BlockSpec(shape, lambda i: (0,) * len(shape))


def shards(
    features,
    stain_delta,
    tissue,
    reduce_weight,
    spatial_weight,
    expand_weight,
    shortcut_weight,
    attn_tanh,
    attn_sigm,
    attn_out,
    classifier,
    step_dir,
):
    rows, cols, chan = features.shape
    mid = reduce_weight.shape[1]
    cout = expand_weight.shape[1]
    att = attn_out.shape[0]
    tiles_r, tiles_c = tissue.shape
    slots = -(-tiles_r * tiles_c // SUB) * SUB
    orow, ocol = rows // 2, cols // 2
    scale = 1.0 + stain_delta
    wide = scale[:, None]
    wr = (reduce_weight.astype(F32) * wide).astype(BF16)
    ws = (shortcut_weight.astype(F32) * wide).astype(BF16)
    wc = spatial_weight.reshape(3, 3 * mid, mid)
    wp = jnp.concatenate([expand_weight, ws], axis=0)
    wb = jnp.concatenate([expand_weight.T, ws.T], axis=1)
    wo = wr.T
    none = jnp.zeros((mid, mid), BF16)

    def turned(a, b):
        return spatial_weight[a, b].T

    wt = jnp.concatenate(
        [
            jnp.concatenate([turned(1, 1), turned(1, 2), turned(2, 1), turned(2, 2)], axis=1),
            jnp.concatenate([none, turned(1, 0), none, turned(2, 0)], axis=1),
            jnp.concatenate([none, none, turned(0, 1), turned(0, 2)], axis=1),
            jnp.concatenate([none, none, none, turned(0, 0)], axis=1),
        ],
        axis=0,
    )
    live = jnp.pad((tissue.reshape(-1, 1) > 0).astype(F32), ((0, slots - tiles_r * tiles_c), (0, 127)))
    ao = attn_out[None, :]
    cls = classifier[None, :]

    rim = dot(jnp.concatenate([features[-1], features[:, -1]], axis=0), wr)
    rim = jax.nn.silu(rim).astype(BF16)
    upper = passed_along(rim[:cols], "space", 1)
    left = passed_along(jnp.concatenate([upper[-1:], rim[cols:]], axis=0), "head", 1).astype(F32)
    up = jnp.concatenate([jnp.zeros((SUB - 1, mid), F32), left[:1], upper.astype(F32)], axis=0)
    left = left[1:, None]

    steps = rows // BLOCK
    params = pltpu.CompilerParams(dimension_semantics=("arbitrary",), vmem_limit_bytes=56 * 1024 * 1024)
    slope1, slope2, slope3, pay, embed, tval, gval, score = pl.pallas_call(
        functools.partial(forward_kernel, tiles_r, tiles_c),
        grid=(steps,),
        out_shape=(
            jax.ShapeDtypeStruct((rows, cols, mid), BF16),
            jax.ShapeDtypeStruct((orow, ocol, mid), BF16),
            jax.ShapeDtypeStruct((orow, ocol, cout), BF16),
            jax.ShapeDtypeStruct((SUB, cout), F32),
            jax.ShapeDtypeStruct((slots, cout), F32),
            jax.ShapeDtypeStruct((slots, att), F32),
            jax.ShapeDtypeStruct((slots, att), F32),
            jax.ShapeDtypeStruct((slots, 128), F32),
        ),
        in_specs=[
            pl.BlockSpec((BLOCK, cols, chan), lambda i: (i, 0, 0)),
            whole(up.shape),
            pl.BlockSpec((BLOCK, 1, mid), lambda i: (i, 0, 0)),
            whole(wr.shape),
            whole(wc.shape),
            whole(wp.shape),
            whole(attn_tanh.shape),
            whole(attn_sigm.shape),
            whole(ao.shape),
            whole(live.shape),
        ],
        out_specs=(
            pl.BlockSpec((BLOCK, cols, mid), lambda i: (i, 0, 0)),
            pl.BlockSpec((BLOCK // 2, ocol, mid), lambda i: (i, 0, 0)),
            pl.BlockSpec((BLOCK // 2, ocol, cout), lambda i: (i, 0, 0)),
            whole((SUB, cout)),
            whole((slots, cout)),
            whole((slots, att)),
            whole((slots, att)),
            whole((slots, 128)),
        ),
        scratch_shapes=[
            pltpu.VMEM((BLOCK, cols + SUB, mid), F32),
            pltpu.VMEM((BLOCK // 2, cols, chan // 2), F32),
            pltpu.VMEM((BLOCK // 2, cols, chan // 2), F32),
            pltpu.VMEM((BLOCK + 1, ocol, 3 * mid), BF16),
            pltpu.VMEM((slots, SUB, cout), F32),
        ],
        compiler_params=params,
        name="forward",
    )(features, up, left, wr, wc, wp, attn_tanh, attn_sigm, ao, live)

    comb = exchange(pay, True, 0)

    we = wb[:, :mid]
    row3, row2, col3, col2 = slope3[:1], slope2[:1], slope3[:, 0], slope2[:, 0]
    dembed, drow, dcol = pl.pallas_call(
        functools.partial(edge_kernel, tiles_r, tiles_c),
        out_shape=(
            jax.ShapeDtypeStruct((slots, cout), F32),
            jax.ShapeDtypeStruct((ocol, mid), BF16),
            jax.ShapeDtypeStruct((orow, mid), BF16),
        ),
        name="edge",
    )(comb, embed, tval, gval, score, live, ao, cls, attn_tanh, attn_sigm, we, row3, row2, col3, col2)
    below = passed_along(drow, "space", -1)
    right = passed_along(jnp.concatenate([dcol, below[:1]], axis=0), "head", -1).astype(F32)
    low = jnp.concatenate([below.astype(F32), right[-1:], jnp.zeros((SUB - 1, mid), F32)], axis=0)
    right = right[:-1, None]

    def turn(i):
        return (steps - 1 - i, 0, 0)

    feature_grad, partial_grad = pl.pallas_call(
        functools.partial(backward_kernel, tiles_c),
        grid=(steps,),
        out_shape=(
            jax.ShapeDtypeStruct((rows, cols, chan), BF16),
            jax.ShapeDtypeStruct((SUB, chan), F32),
        ),
        in_specs=[
            pl.BlockSpec((BLOCK, cols, chan), turn),
            pl.BlockSpec((BLOCK, cols, mid), turn),
            pl.BlockSpec((BLOCK // 2, ocol, mid), turn),
            pl.BlockSpec((BLOCK // 2, ocol, cout), turn),
            whole(dembed.shape),
            pl.BlockSpec((BLOCK // 2, 1, mid), turn),
            whole(low.shape),
            whole(wb.shape),
            whole(wt.shape),
            whole(wo.shape),
        ],
        out_specs=(pl.BlockSpec((BLOCK, cols, chan), turn), whole((SUB, chan))),
        scratch_shapes=[
            pltpu.VMEM((BLOCK // 2 + 1, ocol + SUB, mid), F32),
            pltpu.VMEM((BLOCK, cols, mid), F32),
            pltpu.VMEM((BLOCK // 2, cols, chan // 2), F32),
            pltpu.VMEM((BLOCK // 2, cols, chan // 2), F32),
        ],
        compiler_params=params,
        name="backward",
    )(features, slope1, slope2, slope3, dembed, right, low, wb, wt, wo)

    ddelta = jnp.sum(exchange(partial_grad, False, 1), axis=0) / scale
    norm_size = jnp.sqrt(jnp.mean(ddelta * ddelta) + 1e-06)
    direction = (2 * step_dir - 1).astype(F32)
    new_delta = stain_delta + direction * float(ALPHA) * ddelta / norm_size
    return (feature_grad, new_delta)


def solution(mesh):
    return jax.shard_map(
        shards,
        mesh=mesh,
        in_specs=(P("space", "head", None), P(), P("space", "head")) + (P(),) * 9,
        out_specs=(P("space", "head", None), P()),
        check_vma=False,
    )
```

```python
import functools

import jax
import jax.numpy as jnp
from jax import lax
from jax.experimental import pallas as pl
from jax.experimental.pallas import tpu as pltpu
from jax.sharding import PartitionSpec as P

TILE = 64
ALPHA = 1
BLOCK = 16
SUB = 8
F32 = jnp.float32
MESH = pl.DeviceIdType.MESH
BF16 = jnp.bfloat16
HP = lax.Precision.HIGHEST


def sigm(value):
    return 0.5 + 0.5 * jnp.tanh(0.5 * value)


def passed_along(value, axis, steps):
    count = lax.axis_size(axis)
    first, last = (max(0, -steps), min(count, count - steps))
    return lax.ppermute(value, axis, [(source, source + steps) for source in range(first, last)])


def dot(a, b):
    return jnp.dot(a, b, preferred_element_type=F32)


def column(row, width):
    return jnp.transpose(jnp.broadcast_to(row, (width, row.shape[1])))


def rim_kernel(row_ref, col_ref, delta_ref, w_ref, row_out, col_out, corner_out):
    mid = w_ref.shape[1]
    wr = (w_ref[...].astype(F32) * column(1.0 + delta_ref[...], mid)).astype(BF16)
    row = dot(row_ref[0], wr)
    row = (row * sigm(row)).astype(BF16)
    row_out[...] = row
    corner_out[...] = row[-2 * SUB :]
    col = col_ref[:, SUB:, :].astype(F32)[:, SUB - 1, :].astype(BF16)
    col = dot(col, wr)
    col_out[...] = (col * sigm(col)).astype(BF16)


def turned(weight):
    return jnp.transpose(weight.astype(F32)).astype(BF16)


def weights_kernel(delta_ref, wr_ref, ws_ref, we_ref, sp_ref, wr_out, wp_out, wb_out, wt_out, wo_out):
    mid, cout = we_ref.shape
    wide = column(1.0 + delta_ref[...], mid)
    wr = wr_ref[...].astype(F32) * wide
    wr_out[...] = wr.astype(BF16)
    wo_out[...] = turned(wr)
    wp_out[:mid, :] = we_ref[...]
    wb_out[:, :mid] = turned(we_ref[...])
    for k in range(cout // mid):
        at = slice(k * mid, (k + 1) * mid)
        ws = ws_ref[:, at].astype(F32) * wide
        wp_out[mid:, at] = ws.astype(BF16)
        wb_out[at, mid:] = turned(ws)
    taps = (
        ((1, 1), (1, 2), (2, 1), (2, 2)),
        (None, (1, 0), None, (2, 0)),
        (None, None, (0, 1), (0, 2)),
        (None, None, None, (0, 0)),
    )
    for i, line in enumerate(taps):
        for j, tap in enumerate(line):
            value = jnp.zeros((mid, mid), BF16) if tap is None else turned(sp_ref[tap[0], tap[1]])
            wt_out[i * mid : (i + 1) * mid, j * mid : (j + 1) * mid] = value


def forward_kernel(
    tiles_r, tiles_c, x_ref, up_ref, corner_ref, left_ref, wr_ref, wc_ref, wp_ref, at_ref, as_ref, ao_ref, live_ref,
    slope1_ref, slope2_ref, slope3_ref, row2_ref, row3_ref, col2_ref, col3_ref,
    pay_ref, embed_ref, tval_ref, gval_ref, score_ref,
    red, lo, hi, taps, sums,
):
    step = pl.program_id(0)
    rows, cols, chan = x_ref.shape
    mid = wr_ref.shape[1]
    cout = wp_ref.shape[1]
    orow, ocol = rows // 2, cols // 2
    half = TILE // 2

    def put_taps(slot, source):
        for b, start in enumerate((SUB - 1, SUB, SUB + 1)):
            taps[slot, :, b * mid : (b + 1) * mid] = source[pl.ds(start, ocol, stride=2), :].astype(BF16)

    @pl.when(step == 0)
    def _():
        red[0, SUB - 1 : SUB, :] = corner_ref[...].astype(F32)[-1:]
        red[0, SUB:, :] = up_ref[...].astype(F32)
        put_taps(0, red.at[0])
        sums[...] = jnp.zeros_like(sums)

    @pl.when(step > 0)
    def _():
        taps[0] = taps[rows]

    pre = dot(x_ref[...].reshape(rows * cols, chan), wr_ref[...])
    sig = sigm(pre)
    act = pre * sig
    slope1_ref[...] = (sig + act * (1.0 - sig)).reshape(rows, cols, mid).astype(BF16)
    red[:, SUB:, :] = act.reshape(rows, cols, mid)
    left = left_ref[...].astype(F32)
    for r in range(rows):
        red[r, SUB - 1 : SUB, :] = left[r : r + 1]
        put_taps(r + 1, red.at[r])
    acc = jnp.zeros((orow * ocol, mid), F32)
    for a in range(3):
        part = jnp.stack([taps[2 * i + a] for i in range(orow)], axis=0)
        acc = acc + dot(part.reshape(orow * ocol, 3 * mid), wc_ref[a])
    sig = sigm(acc)
    act = acc * sig
    slope2 = (sig + act * (1.0 - sig)).reshape(orow, ocol, mid)
    slope2_ref[...] = slope2.astype(BF16)
    col2_ref[...] = slope2[:, 0, :]
    short = []
    for i in range(orow):
        lo[i] = x_ref[2 * i, :, : chan // 2].astype(F32)
        hi[i] = x_ref[2 * i, :, chan // 2 :].astype(F32)
    for i in range(orow):
        short.append(
            jnp.concatenate(
                [lo.at[i][pl.ds(0, ocol, stride=2), :].astype(BF16), hi.at[i][pl.ds(0, ocol, stride=2), :].astype(BF16)],
                axis=1,
            )
        )
    short = jnp.stack(short, axis=0).reshape(orow * ocol, chan)
    preact = dot(jnp.concatenate([act.astype(BF16), short], axis=1), wp_ref[...])
    sig = sigm(preact)
    act = preact * sig
    slope3 = (sig + act * (1.0 - sig)).reshape(orow, ocol, cout)
    slope3_ref[...] = slope3.astype(BF16)
    col3_ref[...] = slope3[:, 0, :]

    @pl.when(step == 0)
    def _():
        row2_ref[...] = slope2_ref[0]
        row3_ref[...] = slope3_ref[0]

    cells = jnp.sum(act.reshape(orow, tiles_c, half // SUB, SUB, cout), axis=(0, 2))
    trow = (step * orow) // half
    for c in range(tiles_c):
        slot = trow * tiles_c + c
        sums[slot] = sums[slot] + cells[c]

    @pl.when(step == pl.num_programs(0) - 1)
    def _():
        embed = jnp.sum(sums[...], axis=1) * (1.0 / (half * half))
        tval = jnp.tanh(jnp.dot(embed, at_ref[...], precision=HP, preferred_element_type=F32))
        gval = sigm(jnp.dot(embed, as_ref[...], precision=HP, preferred_element_type=F32))
        score = jnp.sum(tval * gval * ao_ref[...], axis=1, keepdims=True)
        live = live_ref[:, 0:1] > 0
        top = jnp.max(jnp.where(live, score, -1e30), axis=0, keepdims=True)
        weight = jnp.where(live, jnp.exp(score - top), 0.0)
        vector = jnp.sum(weight * embed, axis=0, keepdims=True)
        lines = cout // 128
        for k in range(lines):
            pay_ref[k : k + 1, :] = vector[:, k * 128 : (k + 1) * 128]
        pay_ref[lines : lines + 1, :] = jnp.broadcast_to(jnp.sum(weight, axis=0, keepdims=True), (1, 128))
        pay_ref[lines + 1 : lines + 2, :] = jnp.broadcast_to(top, (1, 128))
        pay_ref[lines + 2 :, :] = jnp.zeros((SUB - lines - 2, 128), F32)
        embed_ref[...] = embed
        tval_ref[...] = tval
        gval_ref[...] = gval
        score_ref[...] = jnp.broadcast_to(score, score_ref.shape)


AXES = ("head", "space")


def peer(sizes, k, hop):
    place = tuple(lax.axis_index(axis) for axis in AXES)
    other = lax.rem(place[k] + hop, sizes[k])
    return (other, place[1]) if k == 0 else (place[0], other)


def corner_of(sizes, hop):
    return tuple(lax.rem(lax.axis_index(axis) + n + hop, n) for axis, n in zip(AXES, sizes))


def greet(sizes, corners):
    barrier = pltpu.get_barrier_semaphore()
    count = 0
    for k in range(2):
        for hop in range(1, sizes[k]):
            pl.semaphore_signal(barrier, inc=1, device_id=peer(sizes, k, hop), device_id_type=MESH)
            count += 1
    if corners:
        for hop in (-1, 1):
            pl.semaphore_signal(barrier, inc=1, device_id=corner_of(sizes, hop), device_id_type=MESH)
            count += 1
    pl.semaphore_wait(barrier, count)


def exchanged(sizes, first, combine, rooms):
    got0, got1, mine, send0, send1, recv0, recv1 = rooms
    mine[0] = first
    for k in range(2):
        got, send, recv = (got0, got1)[k], (send0, send1)[k], (recv0, recv1)[k]
        copies = [
            pltpu.make_async_remote_copy(
                src_ref=mine.at[k],
                dst_ref=got.at[hop],
                send_sem=send.at[hop],
                recv_sem=recv.at[hop],
                device_id=peer(sizes, k, hop),
                device_id_type=MESH,
            )
            for hop in range(1, sizes[k])
        ]
        for copy in copies:
            copy.start()
        got[0] = mine[k]
        for copy in copies:
            copy.wait()
        result = combine(got[...])
        if k == 0:
            mine[1] = result
    return result


def exchange_rooms(sizes):
    shape = (SUB, 128)
    return [
        pltpu.VMEM((sizes[0],) + shape, F32),
        pltpu.VMEM((sizes[1],) + shape, F32),
        pltpu.VMEM((2,) + shape, F32),
        pltpu.SemaphoreType.DMA((sizes[0],)),
        pltpu.SemaphoreType.DMA((sizes[1],)),
        pltpu.SemaphoreType.DMA((sizes[0],)),
        pltpu.SemaphoreType.DMA((sizes[1],)),
    ]


def step_kernel(sizes, grad_ref, delta_ref, dir_ref, out_ref, *rooms):
    greet(sizes, False)
    chan = grad_ref.shape[1]
    lines = chan // 128
    part = jnp.sum(grad_ref[...], axis=0, keepdims=True)
    part = [part[:, k * 128 : (k + 1) * 128] for k in range(lines)]
    part = jnp.concatenate(part + [jnp.zeros((SUB - lines, 128), F32)], axis=0)
    total = exchanged(sizes, part, lambda every: jnp.sum(every, axis=0), rooms)
    delta = delta_ref[...]
    ddelta = jnp.concatenate([total[k : k + 1] for k in range(lines)], axis=1) / (1.0 + delta)
    norm = jnp.sqrt(jnp.sum(ddelta * ddelta, axis=1, keepdims=True) * (1.0 / chan) + 1e-06)
    out_ref[...] = delta + (2 * dir_ref[...] - 1).astype(F32) * float(ALPHA) * ddelta / norm


def spread(dembed_ref, first, tiles_c, half):
    cout = dembed_ref.shape[1]
    return jnp.concatenate(
        [jnp.broadcast_to(dembed_ref[pl.ds(first + c, 1), :], (half, cout)) for c in range(tiles_c)], axis=0
    )


def edge_kernel(
    sizes, tiles_r, tiles_c, pay_ref, embed_ref, tval_ref, gval_ref, score_ref, live_ref, ao_ref, cls_ref, at_ref, as_ref,
    wb_ref, row3_ref, row2_ref, col3_ref, col2_ref, dembed_ref, low_ref, right_ref,
    edges, landed, edge_send, edge_recv, *rooms,
):
    half = TILE // 2
    cout = embed_ref.shape[1]
    lines = cout // 128
    greet(sizes, True)

    def combine(every):
        top = jnp.max(every[:, lines + 1 : lines + 2, :], axis=0)
        factor = jnp.exp(every[:, lines + 1 : lines + 2, :] - top[None])
        total = jnp.sum(every[:, : lines + 1, :] * factor, axis=0)
        return jnp.concatenate([total, top, jnp.zeros((SUB - lines - 2, 128), F32)], axis=0)

    comb = exchanged(sizes, pay_ref[...], combine, rooms)
    total, top = comb[lines : lines + 1, 0:1], comb[lines + 1 : lines + 2, 0:1]
    pooled = jnp.concatenate([comb[k : k + 1] for k in range(lines)], axis=1) / total
    embed, tval, gval = embed_ref[...], tval_ref[...], gval_ref[...]
    ao, cls = ao_ref[...], cls_ref[...]
    live = live_ref[:, 0:1] > 0
    prob = jnp.where(live, jnp.exp(score_ref[:, 0:1] - top), 0.0) / total
    gap = jnp.sum(embed * cls, axis=1, keepdims=True) - jnp.sum(pooled * cls, axis=1, keepdims=True)
    datt = (prob * gap) * ao
    dtanh = datt * gval * (1.0 - tval * tval)
    dsigm = datt * tval * gval * (1.0 - gval)
    back = (((1,), (1,)), ((), ()))
    dembed = (
        prob * cls
        + lax.dot_general(dtanh, at_ref[...], back, precision=HP, preferred_element_type=F32)
        + lax.dot_general(dsigm, as_ref[...], back, precision=HP, preferred_element_type=F32)
    ) * (1.0 / (half * half))
    dembed_ref[...] = dembed
    ocol, mid = row2_ref.shape
    orow = col2_ref.shape[0]
    we = wb_ref[:, :mid]

    def spread_rows(rows):
        return jnp.concatenate([jnp.broadcast_to(dembed[t : t + 1], (half, cout)) for t in rows], axis=0)

    dpre = (row3_ref[...].astype(F32) * spread_rows(range(tiles_c))).astype(BF16)
    edges[0:ocol, :] = (dot(dpre, we) * row2_ref[...].astype(F32)).astype(BF16)
    dpre = (col3_ref[...] * spread_rows(range(0, tiles_r * tiles_c, tiles_c))).astype(BF16)
    edges[ocol : ocol + orow, :] = (dot(dpre, we) * col2_ref[...]).astype(BF16)
    spans = ((0, ocol, 0), (ocol, orow, ocol), (0, 2 * SUB, ocol + orow))
    targets = (peer(sizes, 1, sizes[1] - 1), peer(sizes, 0, sizes[0] - 1), corner_of(sizes, -1))
    copies = [
        pltpu.make_async_remote_copy(
            src_ref=edges.at[pl.ds(source, size)],
            dst_ref=landed.at[pl.ds(place, size)],
            send_sem=edge_send.at[k],
            recv_sem=edge_recv.at[k],
            device_id=targets[k],
            device_id_type=MESH,
        )
        for k, (source, size, place) in enumerate(spans)
    ]
    for copy in copies:
        copy.start()
    for copy in copies:
        copy.wait()
    inner = [lax.axis_index(axis) < n - 1 for axis, n in zip(AXES, sizes)]
    below = jnp.where(inner[1], 1.0, 0.0)
    beside = jnp.where(inner[0], 1.0, 0.0)
    low_ref[0:ocol, :] = landed[0:ocol, :].astype(F32) * below
    right_ref[...] = landed[ocol : ocol + orow, :].astype(F32) * beside
    low_ref[ocol:, :] = landed[ocol + orow :, :].astype(F32)[:SUB] * (below * beside)


def backward_kernel(
    tiles_c, x_ref, slope1_ref, slope2_ref, slope3_ref, dembed_ref, right_ref, low_ref, wb_ref, wt_ref, wo_ref,
    out_ref, grad_ref, dsx, drs, slo, shi,
):
    step = pl.program_id(0)
    rows, cols, chan = x_ref.shape
    orow, ocol, mid = slope2_ref.shape
    cout = slope3_ref.shape[2]
    half = TILE // 2
    block = pl.num_programs(0) - 1 - step
    trow = (block * orow) // half

    @pl.when(step == 0)
    def _():
        dsx[orow, :, :] = low_ref[...]
        slo[...] = jnp.zeros_like(slo)
        shi[...] = jnp.zeros_like(shi)
        grad_ref[...] = jnp.zeros_like(grad_ref)

    @pl.when(step > 0)
    def _():
        dsx[orow] = dsx[0]

    dpre = (slope3_ref[...].astype(F32) * spread(dembed_ref, trow * tiles_c, tiles_c, half)[None]).astype(BF16)
    both = dot(dpre.reshape(orow * ocol, cout), wb_ref[...])
    dsx[0:orow, 0:ocol, :] = both[:, :mid].reshape(orow, ocol, mid) * slope2_ref[...].astype(F32)
    for i in range(orow):
        dsx[i, ocol : ocol + 1, :] = right_ref[i : i + 1, :]
        slo[i, pl.ds(0, ocol, stride=2), :] = both[i * ocol : (i + 1) * ocol, mid : mid + chan // 2]
        shi[i, pl.ds(0, ocol, stride=2), :] = both[i * ocol : (i + 1) * ocol, mid + chan // 2 :]
    four = jnp.concatenate(
        [
            dsx[di : di + orow, dj : dj + ocol, :].astype(BF16).reshape(orow * ocol, mid)
            for di in range(2)
            for dj in range(2)
        ],
        axis=1,
    )
    grads = dot(four, wt_ref[...])
    for i in range(orow):
        for di in range(2):
            for dj in range(2):
                n = 2 * di + dj
                drs[2 * i + di, pl.ds(dj, ocol, stride=2), :] = grads[i * ocol : (i + 1) * ocol, n * mid : (n + 1) * mid]
    dred = (drs[...] * slope1_ref[...].astype(F32)).astype(BF16)
    dinput = dot(dred.reshape(rows * cols, mid), wo_ref[...]).reshape(rows, cols, chan)
    total = jnp.zeros((SUB, chan), F32)
    for r in range(rows):
        value = dinput[r]
        if r % 2 == 0:
            value = value + jnp.concatenate([slo[r // 2], shi[r // 2]], axis=1)
        out_ref[r] = value.astype(BF16)
        total = total + jnp.sum((value * x_ref[r].astype(F32)).reshape(cols // SUB, SUB, chan), axis=0)
    grad_ref[...] += total


def whole(shape):
    return pl.BlockSpec(shape, lambda i: (0,) * len(shape))


def shards(
    features,
    stain_delta,
    tissue,
    reduce_weight,
    spatial_weight,
    expand_weight,
    shortcut_weight,
    attn_tanh,
    attn_sigm,
    attn_out,
    classifier,
    step_dir,
):
    rows, cols, chan = features.shape
    mid = reduce_weight.shape[1]
    cout = expand_weight.shape[1]
    att = attn_out.shape[0]
    tiles_r, tiles_c = tissue.shape
    slots = -(-tiles_r * tiles_c // SUB) * SUB
    orow, ocol = rows // 2, cols // 2
    delta = stain_delta[None, :]
    wc = spatial_weight.reshape(3, 3 * mid, mid)
    live = jnp.pad((tissue.reshape(-1, 1) > 0).astype(F32), ((0, slots - tiles_r * tiles_c), (0, 127)))
    ao = attn_out[None, :]
    cls = classifier[None, :]
    sizes = tuple(lax.axis_size(axis) for axis in AXES)

    rim_row, rim_col, rim_corner = pl.pallas_call(
        rim_kernel,
        grid=(1,),
        out_shape=(
            jax.ShapeDtypeStruct((cols, mid), BF16),
            jax.ShapeDtypeStruct((rows, mid), BF16),
            jax.ShapeDtypeStruct((2 * SUB, mid), BF16),
        ),
        in_specs=[
            pl.BlockSpec((1, cols, chan), lambda i: (rows - 1, 0, 0)),
            pl.BlockSpec((rows, 2 * SUB, chan), lambda i: (0, cols // (2 * SUB) - 1, 0)),
            whole(delta.shape),
            whole(reduce_weight.shape),
        ],
        out_specs=(whole((cols, mid)), whole((rows, mid)), whole((2 * SUB, mid))),
        name="rim",
    )(features, features, delta, reduce_weight)
    up = passed_along(rim_row, "space", 1)
    left = passed_along(rim_col, "head", 1)
    corner = lax.ppermute(
        rim_corner,
        AXES,
        [
            (h * sizes[1] + s, (h + 1) * sizes[1] + s + 1)
            for h in range(sizes[0] - 1)
            for s in range(sizes[1] - 1)
        ],
    )
    wr, wp, wb, wt, wo = pl.pallas_call(
        weights_kernel,
        out_shape=(
            jax.ShapeDtypeStruct((chan, mid), BF16),
            jax.ShapeDtypeStruct((mid + chan, cout), BF16),
            jax.ShapeDtypeStruct((cout, mid + chan), BF16),
            jax.ShapeDtypeStruct((4 * mid, 4 * mid), BF16),
            jax.ShapeDtypeStruct((mid, chan), BF16),
        ),
        cost_estimate=pl.CostEstimate(flops=10**8, bytes_accessed=8 * 10**6, transcendentals=0),
        name="weights",
    )(delta, reduce_weight, shortcut_weight, expand_weight, spatial_weight)

    steps = rows // BLOCK
    params = pltpu.CompilerParams(dimension_semantics=("arbitrary",), vmem_limit_bytes=56 * 1024 * 1024)
    slope1, slope2, slope3, row2, row3, col2, col3, pay, embed, tval, gval, score = pl.pallas_call(
        functools.partial(forward_kernel, tiles_r, tiles_c),
        grid=(steps,),
        out_shape=(
            jax.ShapeDtypeStruct((rows, cols, mid), BF16),
            jax.ShapeDtypeStruct((orow, ocol, mid), BF16),
            jax.ShapeDtypeStruct((orow, ocol, cout), BF16),
            jax.ShapeDtypeStruct((ocol, mid), BF16),
            jax.ShapeDtypeStruct((ocol, cout), BF16),
            jax.ShapeDtypeStruct((orow, mid), F32),
            jax.ShapeDtypeStruct((orow, cout), F32),
            jax.ShapeDtypeStruct((SUB, 128), F32),
            jax.ShapeDtypeStruct((slots, cout), F32),
            jax.ShapeDtypeStruct((slots, att), F32),
            jax.ShapeDtypeStruct((slots, att), F32),
            jax.ShapeDtypeStruct((slots, 128), F32),
        ),
        in_specs=[
            pl.BlockSpec((BLOCK, cols, chan), lambda i: (i, 0, 0)),
            whole(up.shape),
            whole(corner.shape),
            pl.BlockSpec((BLOCK, mid), lambda i: (i, 0)),
            whole(wr.shape),
            whole(wc.shape),
            whole(wp.shape),
            whole(attn_tanh.shape),
            whole(attn_sigm.shape),
            whole(ao.shape),
            whole(live.shape),
        ],
        out_specs=(
            pl.BlockSpec((BLOCK, cols, mid), lambda i: (i, 0, 0)),
            pl.BlockSpec((BLOCK // 2, ocol, mid), lambda i: (i, 0, 0)),
            pl.BlockSpec((BLOCK // 2, ocol, cout), lambda i: (i, 0, 0)),
            whole((ocol, mid)),
            whole((ocol, cout)),
            pl.BlockSpec((BLOCK // 2, mid), lambda i: (i, 0)),
            pl.BlockSpec((BLOCK // 2, cout), lambda i: (i, 0)),
            whole((SUB, 128)),
            whole((slots, cout)),
            whole((slots, att)),
            whole((slots, att)),
            whole((slots, 128)),
        ),
        scratch_shapes=[
            pltpu.VMEM((BLOCK, cols + SUB, mid), F32),
            pltpu.VMEM((BLOCK // 2, cols, chan // 2), F32),
            pltpu.VMEM((BLOCK // 2, cols, chan // 2), F32),
            pltpu.VMEM((BLOCK + 1, ocol, 3 * mid), BF16),
            pltpu.VMEM((slots, SUB, cout), F32),
        ],
        compiler_params=params,
        name="forward",
    )(features, up, corner, left, wr, wc, wp, attn_tanh, attn_sigm, ao, live)

    dembed, low, right = pl.pallas_call(
        functools.partial(edge_kernel, sizes, tiles_r, tiles_c),
        out_shape=(
            jax.ShapeDtypeStruct((slots, cout), F32),
            jax.ShapeDtypeStruct((ocol + SUB, mid), F32),
            jax.ShapeDtypeStruct((orow, mid), F32),
        ),
        scratch_shapes=[
            pltpu.VMEM((ocol + orow, mid), BF16),
            pltpu.VMEM((ocol + orow + 2 * SUB, mid), BF16),
            pltpu.SemaphoreType.DMA((3,)),
            pltpu.SemaphoreType.DMA((3,)),
        ]
        + exchange_rooms(sizes),
        compiler_params=pltpu.CompilerParams(collective_id=0, has_side_effects=True),
        name="edge",
    )(pay, embed, tval, gval, score, live, ao, cls, attn_tanh, attn_sigm, wb, row3, row2, col3, col2)

    def turn(i):
        return (steps - 1 - i, 0, 0)

    feature_grad, partial_grad = pl.pallas_call(
        functools.partial(backward_kernel, tiles_c),
        grid=(steps,),
        out_shape=(
            jax.ShapeDtypeStruct((rows, cols, chan), BF16),
            jax.ShapeDtypeStruct((SUB, chan), F32),
        ),
        in_specs=[
            pl.BlockSpec((BLOCK, cols, chan), turn),
            pl.BlockSpec((BLOCK, cols, mid), turn),
            pl.BlockSpec((BLOCK // 2, ocol, mid), turn),
            pl.BlockSpec((BLOCK // 2, ocol, cout), turn),
            whole(dembed.shape),
            pl.BlockSpec((BLOCK // 2, mid), lambda i: (steps - 1 - i, 0)),
            whole(low.shape),
            whole(wb.shape),
            whole(wt.shape),
            whole(wo.shape),
        ],
        out_specs=(pl.BlockSpec((BLOCK, cols, chan), turn), whole((SUB, chan))),
        scratch_shapes=[
            pltpu.VMEM((BLOCK // 2 + 1, ocol + SUB, mid), F32),
            pltpu.VMEM((BLOCK, cols, mid), F32),
            pltpu.VMEM((BLOCK // 2, cols, chan // 2), F32),
            pltpu.VMEM((BLOCK // 2, cols, chan // 2), F32),
        ],
        compiler_params=params,
        name="backward",
    )(features, slope1, slope2, slope3, dembed, right, low, wb, wt, wo)

    new_delta = pl.pallas_call(
        functools.partial(step_kernel, sizes),
        out_shape=jax.ShapeDtypeStruct((1, chan), F32),
        scratch_shapes=exchange_rooms(sizes),
        compiler_params=pltpu.CompilerParams(collective_id=1, has_side_effects=True),
        name="step",
    )(partial_grad, delta, step_dir[None, :])[0]
    return (feature_grad, new_delta)


def solution(mesh):
    return jax.shard_map(
        shards,
        mesh=mesh,
        in_specs=(P("space", "head", None), P(), P("space", "head")) + (P(),) * 9,
        out_specs=(P("space", "head", None), P()),
        check_vma=False,
    )
```

```python
import functools

import jax
import jax.numpy as jnp
from jax import lax
from jax.experimental import pallas as pl
from jax.experimental.pallas import tpu as pltpu
from jax.sharding import PartitionSpec as P

TILE = 64
ALPHA = 1
BLOCK = 32
SUB = 8
F32 = jnp.float32
MESH = pl.DeviceIdType.MESH
BF16 = jnp.bfloat16
HP = lax.Precision.HIGHEST


def sigm(value):
    return 0.5 + 0.5 * jnp.tanh(0.5 * value)


def dot(a, b):
    return jnp.dot(a, b, preferred_element_type=F32)


def column(row, width):
    return jnp.transpose(jnp.broadcast_to(row, (width, row.shape[1])))


def turned(weight):
    return jnp.transpose(weight.astype(F32)).astype(BF16)


def forward_kernel(
    tiles_r, tiles_c, x_ref, up_ref, left_ref, wr_ref, wc_ref, wp_ref, at_ref, as_ref, ao_ref, live_ref,
    slope1_ref, slope2_ref, slope3_ref, row2_ref, row3_ref, col2_ref, col3_ref,
    pay_ref, embed_ref, tval_ref, gval_ref, score_ref,
    red, lo, hi, taps, sums,
):
    step = pl.program_id(0)
    rows, cols, chan = x_ref.shape
    mid = wr_ref.shape[1]
    cout = wp_ref.shape[1]
    orow, ocol = rows // 2, cols // 2
    half = TILE // 2

    def put_taps(slot, source):
        for b, start in enumerate((SUB - 1, SUB, SUB + 1)):
            taps[slot, :, b * mid : (b + 1) * mid] = source[pl.ds(start, ocol, stride=2), :].astype(BF16)

    @pl.when(step == 0)
    def _():
        put_taps(0, up_ref)
        sums[...] = jnp.zeros_like(sums)

    @pl.when(step > 0)
    def _():
        taps[0] = taps[rows]

    pre = dot(x_ref[...].reshape(rows * cols, chan), wr_ref[...])
    sig = sigm(pre)
    act = pre * sig
    slope1_ref[...] = (sig + act * (1.0 - sig)).reshape(rows, cols, mid).astype(BF16)
    red[:, SUB:, :] = act.reshape(rows, cols, mid)
    for r in range(rows):
        red[r, SUB - 1 : SUB, :] = left_ref[r : r + 1, :]
        put_taps(r + 1, red.at[r])
    acc = jnp.zeros((orow * ocol, mid), F32)
    for a in range(3):
        part = jnp.stack([taps[2 * i + a] for i in range(orow)], axis=0)
        acc = acc + dot(part.reshape(orow * ocol, 3 * mid), wc_ref[a])
    sig = sigm(acc)
    act = acc * sig
    slope2 = (sig + act * (1.0 - sig)).reshape(orow, ocol, mid)
    slope2_ref[...] = slope2.astype(BF16)
    col2_ref[...] = slope2[:, 0, :]
    short = []
    for i in range(orow):
        lo[i] = x_ref[2 * i, :, : chan // 2].astype(F32)
        hi[i] = x_ref[2 * i, :, chan // 2 :].astype(F32)
    for i in range(orow):
        short.append(
            jnp.concatenate(
                [lo.at[i][pl.ds(0, ocol, stride=2), :].astype(BF16), hi.at[i][pl.ds(0, ocol, stride=2), :].astype(BF16)],
                axis=1,
            )
        )
    short = jnp.stack(short, axis=0).reshape(orow * ocol, chan)
    preact = dot(jnp.concatenate([act.astype(BF16), short], axis=1), wp_ref[...])
    sig = sigm(preact)
    act = preact * sig
    slope3 = (sig + act * (1.0 - sig)).reshape(orow, ocol, cout)
    slope3_ref[...] = slope3.astype(BF16)
    col3_ref[...] = slope3[:, 0, :]

    @pl.when(step == 0)
    def _():
        row2_ref[...] = slope2_ref[0]
        row3_ref[...] = slope3_ref[0]

    cells = jnp.sum(act.reshape(orow, tiles_c, half // SUB, SUB, cout), axis=(0, 2))
    trow = (step * orow) // half
    for c in range(tiles_c):
        slot = trow * tiles_c + c
        sums[slot] = sums[slot] + cells[c]

    @pl.when(step == pl.num_programs(0) - 1)
    def _():
        embed = jnp.sum(sums[...], axis=1) * (1.0 / (half * half))
        tval = jnp.tanh(jnp.dot(embed, at_ref[...], precision=HP, preferred_element_type=F32))
        gval = sigm(jnp.dot(embed, as_ref[...], precision=HP, preferred_element_type=F32))
        score = jnp.sum(tval * gval * ao_ref[...], axis=1, keepdims=True)
        live = live_ref[:, 0:1] > 0
        top = jnp.max(jnp.where(live, score, -1e30), axis=0, keepdims=True)
        weight = jnp.where(live, jnp.exp(score - top), 0.0)
        vector = jnp.sum(weight * embed, axis=0, keepdims=True)
        lines = cout // 128
        for k in range(lines):
            pay_ref[k : k + 1, :] = vector[:, k * 128 : (k + 1) * 128]
        pay_ref[lines : lines + 1, :] = jnp.broadcast_to(jnp.sum(weight, axis=0, keepdims=True), (1, 128))
        pay_ref[lines + 1 : lines + 2, :] = jnp.broadcast_to(top, (1, 128))
        pay_ref[lines + 2 :, :] = jnp.zeros((SUB - lines - 2, 128), F32)
        embed_ref[...] = embed
        tval_ref[...] = tval
        gval_ref[...] = gval
        score_ref[...] = jnp.where(live, jnp.broadcast_to(score, score_ref.shape), -1e30)


AXES = ("head", "space")


def peer(sizes, k, hop):
    place = tuple(lax.axis_index(axis) for axis in AXES)
    other = lax.rem(place[k] + hop, sizes[k])
    return (other, place[1]) if k == 0 else (place[0], other)


def corner_of(sizes, hop):
    return tuple(lax.rem(lax.axis_index(axis) + n + hop, n) for axis, n in zip(AXES, sizes))


def greet(sizes, corners):
    barrier = pltpu.get_barrier_semaphore()
    count = 0
    for k in range(2):
        for hop in range(1, sizes[k]):
            pl.semaphore_signal(barrier, inc=1, device_id=peer(sizes, k, hop), device_id_type=MESH)
            count += 1
    if corners:
        for hop in (-1, 1):
            pl.semaphore_signal(barrier, inc=1, device_id=corner_of(sizes, hop), device_id_type=MESH)
            count += 1
    pl.semaphore_wait(barrier, count)


def exchanged(sizes, first, combine, rooms):
    got0, got1, mine, send0, send1, recv0, recv1 = rooms
    mine[0] = first
    for k in range(2):
        got, send, recv = (got0, got1)[k], (send0, send1)[k], (recv0, recv1)[k]
        copies = [
            pltpu.make_async_remote_copy(
                src_ref=mine.at[k],
                dst_ref=got.at[hop],
                send_sem=send.at[hop],
                recv_sem=recv.at[hop],
                device_id=peer(sizes, k, hop),
                device_id_type=MESH,
            )
            for hop in range(1, sizes[k])
        ]
        for copy in copies:
            copy.start()
        got[0] = mine[k]
        for copy in copies:
            copy.wait()
        result = combine(got[...])
        if k == 0:
            mine[1] = result
    return result


def exchange_rooms(sizes):
    shape = (SUB, 128)
    return [
        pltpu.VMEM((sizes[0],) + shape, F32),
        pltpu.VMEM((sizes[1],) + shape, F32),
        pltpu.VMEM((2,) + shape, F32),
        pltpu.SemaphoreType.DMA((sizes[0],)),
        pltpu.SemaphoreType.DMA((sizes[1],)),
        pltpu.SemaphoreType.DMA((sizes[0],)),
        pltpu.SemaphoreType.DMA((sizes[1],)),
    ]


def rim_kernel(
    sizes, row_ref, col_ref, delta_ref, wr_ref, ws_ref, we_ref, sp_ref,
    up_out, left_out, wr_out, wp_out, wb_out, wt_out, wo_out,
    edges, landed, edge_send, edge_recv,
):
    targets = (peer(sizes, 1, 1), peer(sizes, 0, 1), corner_of(sizes, 1))
    sources = (peer(sizes, 1, sizes[1] - 1), peer(sizes, 0, sizes[0] - 1), corner_of(sizes, -1))
    barrier = pltpu.get_barrier_semaphore()
    for device in targets + sources:
        pl.semaphore_signal(barrier, inc=1, device_id=device, device_id_type=MESH)
    mid, cout = we_ref.shape
    cols, rows = row_ref.shape[1], col_ref.shape[0]
    wide = column(1.0 + delta_ref[...], mid)
    wr = wr_ref[...].astype(F32) * wide
    wr_out[...] = wr.astype(BF16)
    col = col_ref[:, SUB:, :].astype(F32)[:, SUB - 1, :].astype(BF16)
    both = dot(jnp.concatenate([row_ref[0], col], axis=0), wr.astype(BF16))
    edges[...] = (both * sigm(both)).astype(BF16)
    spans = ((0, cols, 0), (cols, rows, cols), (cols - 2 * SUB, 2 * SUB, cols + rows))
    copies = [
        pltpu.make_async_remote_copy(
            src_ref=edges.at[pl.ds(source, size)],
            dst_ref=landed.at[pl.ds(place, size)],
            send_sem=edge_send.at[k],
            recv_sem=edge_recv.at[k],
            device_id=targets[k],
            device_id_type=MESH,
        )
        for k, (source, size, place) in enumerate(spans)
    ]
    pl.semaphore_wait(barrier, 6)
    for copy in copies:
        copy.start()
    wo_out[...] = turned(wr)
    wp_out[:mid, :] = we_ref[...]
    wb_out[:, :mid] = turned(we_ref[...])
    for k in range(cout // mid):
        at = slice(k * mid, (k + 1) * mid)
        ws = ws_ref[:, at].astype(F32) * wide
        wp_out[mid:, at] = ws.astype(BF16)
        wb_out[at, mid:] = turned(ws)
    taps = (
        ((1, 1), (1, 2), (2, 1), (2, 2)),
        (None, (1, 0), None, (2, 0)),
        (None, None, (0, 1), (0, 2)),
        (None, None, None, (0, 0)),
    )
    for i, line in enumerate(taps):
        for j, tap in enumerate(line):
            value = jnp.zeros((mid, mid), BF16) if tap is None else turned(sp_ref[tap[0], tap[1]])
            wt_out[i * mid : (i + 1) * mid, j * mid : (j + 1) * mid] = value
    for copy in copies:
        copy.wait()
    above = jnp.where(lax.axis_index("space") > 0, 1.0, 0.0)
    beside = jnp.where(lax.axis_index("head") > 0, 1.0, 0.0)
    up_out[0:SUB, :] = landed[cols + rows :, :].astype(F32)[SUB:] * (above * beside)
    up_out[SUB:, :] = landed[0:cols, :].astype(F32) * above
    left_out[...] = landed[cols : cols + rows, :].astype(F32) * beside


def step_kernel(sizes, grad_ref, delta_ref, dir_ref, out_ref, *rooms):
    greet(sizes, False)
    chan = grad_ref.shape[1]
    lines = chan // 128
    part = jnp.sum(grad_ref[...], axis=0, keepdims=True)
    part = [part[:, k * 128 : (k + 1) * 128] for k in range(lines)]
    part = jnp.concatenate(part + [jnp.zeros((SUB - lines, 128), F32)], axis=0)
    total = exchanged(sizes, part, lambda every: jnp.sum(every, axis=0), rooms)
    delta = delta_ref[...]
    ddelta = jnp.concatenate([total[k : k + 1] for k in range(lines)], axis=1) / (1.0 + delta)
    norm = jnp.sqrt(jnp.sum(ddelta * ddelta, axis=1, keepdims=True) * (1.0 / chan) + 1e-06)
    out_ref[...] = (2 * dir_ref[...] - 1).astype(F32) * float(ALPHA) * ddelta / norm


def spread(dembed_ref, first, tiles_c, half):
    cout = dembed_ref.shape[1]
    return jnp.concatenate(
        [jnp.broadcast_to(dembed_ref[pl.ds(first + c, 1), :], (half, cout)) for c in range(tiles_c)], axis=0
    )


def edge_kernel(
    sizes, tiles_r, tiles_c, pay_ref, embed_ref, tval_ref, gval_ref, score_ref, live_ref, ao_ref, cls_ref, at_ref, as_ref,
    wb_ref, row3_ref, row2_ref, col3_ref, col2_ref, dembed_ref, low_ref, right_ref,
    edges, landed, edge_send, edge_recv, *rooms,
):
    half = TILE // 2
    cout = embed_ref.shape[1]
    lines = cout // 128
    greet(sizes, True)

    def combine(every):
        top = jnp.max(every[:, lines + 1 : lines + 2, :], axis=0)
        factor = jnp.exp(every[:, lines + 1 : lines + 2, :] - top[None])
        total = jnp.sum(every[:, : lines + 1, :] * factor, axis=0)
        return jnp.concatenate([total, top, jnp.zeros((SUB - lines - 2, 128), F32)], axis=0)

    comb = exchanged(sizes, pay_ref[...], combine, rooms)
    total, top = comb[lines : lines + 1, 0:1], comb[lines + 1 : lines + 2, 0:1]
    pooled = jnp.concatenate([comb[k : k + 1] for k in range(lines)], axis=1) / total
    embed, tval, gval = embed_ref[...], tval_ref[...], gval_ref[...]
    ao, cls = ao_ref[...], cls_ref[...]
    live = live_ref[:, 0:1] > 0
    prob = jnp.where(live, jnp.exp(score_ref[:, 0:1] - top), 0.0) / total
    gap = jnp.sum(embed * cls, axis=1, keepdims=True) - jnp.sum(pooled * cls, axis=1, keepdims=True)
    datt = (prob * gap) * ao
    dtanh = datt * gval * (1.0 - tval * tval)
    dsigm = datt * tval * gval * (1.0 - gval)
    back = (((1,), (1,)), ((), ()))
    dembed = (
        prob * cls
        + lax.dot_general(dtanh, at_ref[...], back, precision=HP, preferred_element_type=F32)
        + lax.dot_general(dsigm, as_ref[...], back, precision=HP, preferred_element_type=F32)
    ) * (1.0 / (half * half))
    dembed_ref[...] = dembed
    ocol, mid = row2_ref.shape
    orow = col2_ref.shape[0]
    we = wb_ref[:, :mid]

    def spread_rows(rows):
        return jnp.concatenate([jnp.broadcast_to(dembed[t : t + 1], (half, cout)) for t in rows], axis=0)

    dpre = (row3_ref[...].astype(F32) * spread_rows(range(tiles_c))).astype(BF16)
    edges[0:ocol, :] = (dot(dpre, we) * row2_ref[...].astype(F32)).astype(BF16)
    dpre = (col3_ref[...] * spread_rows(range(0, tiles_r * tiles_c, tiles_c))).astype(BF16)
    edges[ocol : ocol + orow, :] = (dot(dpre, we) * col2_ref[...]).astype(BF16)
    spans = ((0, ocol, 0), (ocol, orow, ocol), (0, 2 * SUB, ocol + orow))
    targets = (peer(sizes, 1, sizes[1] - 1), peer(sizes, 0, sizes[0] - 1), corner_of(sizes, -1))
    copies = [
        pltpu.make_async_remote_copy(
            src_ref=edges.at[pl.ds(source, size)],
            dst_ref=landed.at[pl.ds(place, size)],
            send_sem=edge_send.at[k],
            recv_sem=edge_recv.at[k],
            device_id=targets[k],
            device_id_type=MESH,
        )
        for k, (source, size, place) in enumerate(spans)
    ]
    for copy in copies:
        copy.start()
    for copy in copies:
        copy.wait()
    inner = [lax.axis_index(axis) < n - 1 for axis, n in zip(AXES, sizes)]
    below = jnp.where(inner[1], 1.0, 0.0)
    beside = jnp.where(inner[0], 1.0, 0.0)
    low_ref[0:ocol, :] = landed[0:ocol, :].astype(F32) * below
    right_ref[...] = landed[ocol : ocol + orow, :].astype(F32) * beside
    low_ref[ocol:, :] = landed[ocol + orow :, :].astype(F32)[:SUB] * (below * beside)


def backward_kernel(
    tiles_c, x_ref, slope1_ref, slope2_ref, slope3_ref, dembed_ref, right_ref, low_ref, wb_ref, wt_ref, wo_ref,
    out_ref, grad_ref, dsx, drs, slo, shi,
):
    step = pl.program_id(0)
    rows, cols, chan = x_ref.shape
    orow, ocol, mid = slope2_ref.shape
    cout = slope3_ref.shape[2]
    half = TILE // 2
    block = pl.num_programs(0) - 1 - step
    trow = (block * orow) // half

    @pl.when(step == 0)
    def _():
        dsx[orow, :, :] = low_ref[...]
        slo[...] = jnp.zeros_like(slo)
        shi[...] = jnp.zeros_like(shi)
        grad_ref[...] = jnp.zeros_like(grad_ref)

    @pl.when(step > 0)
    def _():
        dsx[orow] = dsx[0]

    dpre = (slope3_ref[...].astype(F32) * spread(dembed_ref, trow * tiles_c, tiles_c, half)[None]).astype(BF16)
    both = dot(dpre.reshape(orow * ocol, cout), wb_ref[...])
    dsx[0:orow, 0:ocol, :] = both[:, :mid].reshape(orow, ocol, mid) * slope2_ref[...].astype(F32)
    for i in range(orow):
        dsx[i, ocol : ocol + 1, :] = right_ref[i : i + 1, :]
        slo[i, pl.ds(0, ocol, stride=2), :] = both[i * ocol : (i + 1) * ocol, mid : mid + chan // 2]
        shi[i, pl.ds(0, ocol, stride=2), :] = both[i * ocol : (i + 1) * ocol, mid + chan // 2 :]
    four = jnp.concatenate(
        [
            dsx[di : di + orow, dj : dj + ocol, :].astype(BF16).reshape(orow * ocol, mid)
            for di in range(2)
            for dj in range(2)
        ],
        axis=1,
    )
    grads = dot(four, wt_ref[...])
    for i in range(orow):
        for di in range(2):
            for dj in range(2):
                n = 2 * di + dj
                drs[2 * i + di, pl.ds(dj, ocol, stride=2), :] = grads[i * ocol : (i + 1) * ocol, n * mid : (n + 1) * mid]
    dred = (drs[...] * slope1_ref[...].astype(F32)).astype(BF16)
    dinput = dot(dred.reshape(rows * cols, mid), wo_ref[...]).reshape(rows, cols, chan)
    total = jnp.zeros((SUB, chan), F32)
    for r in range(rows):
        value = dinput[r]
        if r % 2 == 0:
            value = value + jnp.concatenate([slo[r // 2], shi[r // 2]], axis=1)
        out_ref[r] = value.astype(BF16)
        total = total + jnp.sum((value * x_ref[r].astype(F32)).reshape(cols // SUB, SUB, chan), axis=0)
    grad_ref[...] += total


def whole(shape):
    return pl.BlockSpec(shape, lambda i: (0,) * len(shape))


def shards(
    features,
    stain_delta,
    tissue,
    reduce_weight,
    spatial_weight,
    expand_weight,
    shortcut_weight,
    attn_tanh,
    attn_sigm,
    attn_out,
    classifier,
    step_dir,
):
    rows, cols, chan = features.shape
    mid = reduce_weight.shape[1]
    cout = expand_weight.shape[1]
    att = attn_out.shape[0]
    tiles_r, tiles_c = tissue.shape
    slots = -(-tiles_r * tiles_c // SUB) * SUB
    orow, ocol = rows // 2, cols // 2
    delta = stain_delta[None, :]
    wc = spatial_weight.reshape(3, 3 * mid, mid)
    live = jnp.pad((tissue.reshape(-1, 1) > 0).astype(F32), ((0, slots - tiles_r * tiles_c), (0, 127)))
    ao = attn_out[None, :]
    cls = classifier[None, :]
    sizes = tuple(lax.axis_size(axis) for axis in AXES)

    up, left, wr, wp, wb, wt, wo = pl.pallas_call(
        functools.partial(rim_kernel, sizes),
        grid=(1,),
        out_shape=(
            jax.ShapeDtypeStruct((cols + SUB, mid), F32),
            jax.ShapeDtypeStruct((rows, mid), F32),
            jax.ShapeDtypeStruct((chan, mid), BF16),
            jax.ShapeDtypeStruct((mid + chan, cout), BF16),
            jax.ShapeDtypeStruct((cout, mid + chan), BF16),
            jax.ShapeDtypeStruct((4 * mid, 4 * mid), BF16),
            jax.ShapeDtypeStruct((mid, chan), BF16),
        ),
        in_specs=[
            pl.BlockSpec((1, cols, chan), lambda i: (rows - 1, 0, 0)),
            pl.BlockSpec((rows, 2 * SUB, chan), lambda i: (0, cols // (2 * SUB) - 1, 0)),
            whole(delta.shape),
            whole(reduce_weight.shape),
            whole(shortcut_weight.shape),
            whole(expand_weight.shape),
            whole(spatial_weight.shape),
        ],
        out_specs=(
            whole((cols + SUB, mid)),
            whole((rows, mid)),
            whole((chan, mid)),
            whole((mid + chan, cout)),
            whole((cout, mid + chan)),
            whole((4 * mid, 4 * mid)),
            whole((mid, chan)),
        ),
        scratch_shapes=[
            pltpu.VMEM((cols + rows, mid), BF16),
            pltpu.VMEM((cols + rows + 2 * SUB, mid), BF16),
            pltpu.SemaphoreType.DMA((3,)),
            pltpu.SemaphoreType.DMA((3,)),
        ],
        compiler_params=pltpu.CompilerParams(collective_id=2, has_side_effects=True),
        name="rim",
    )(features, features, delta, reduce_weight, shortcut_weight, expand_weight, spatial_weight)

    steps = rows // BLOCK
    params = pltpu.CompilerParams(dimension_semantics=("arbitrary",), vmem_limit_bytes=56 * 1024 * 1024)
    slope1, slope2, slope3, row2, row3, col2, col3, pay, embed, tval, gval, score = pl.pallas_call(
        functools.partial(forward_kernel, tiles_r, tiles_c),
        grid=(steps,),
        out_shape=(
            jax.ShapeDtypeStruct((rows, cols, mid), BF16),
            jax.ShapeDtypeStruct((orow, ocol, mid), BF16),
            jax.ShapeDtypeStruct((orow, ocol, cout), BF16),
            jax.ShapeDtypeStruct((ocol, mid), BF16),
            jax.ShapeDtypeStruct((ocol, cout), BF16),
            jax.ShapeDtypeStruct((orow, mid), F32),
            jax.ShapeDtypeStruct((orow, cout), F32),
            jax.ShapeDtypeStruct((SUB, 128), F32),
            jax.ShapeDtypeStruct((slots, cout), F32),
            jax.ShapeDtypeStruct((slots, att), F32),
            jax.ShapeDtypeStruct((slots, att), F32),
            jax.ShapeDtypeStruct((slots, 128), F32),
        ),
        in_specs=[
            pl.BlockSpec((BLOCK, cols, chan), lambda i: (i, 0, 0)),
            whole(up.shape),
            pl.BlockSpec((BLOCK, mid), lambda i: (i, 0)),
            whole(wr.shape),
            whole(wc.shape),
            whole(wp.shape),
            whole(attn_tanh.shape),
            whole(attn_sigm.shape),
            whole(ao.shape),
            whole(live.shape),
        ],
        out_specs=(
            pl.BlockSpec((BLOCK, cols, mid), lambda i: (i, 0, 0)),
            pl.BlockSpec((BLOCK // 2, ocol, mid), lambda i: (i, 0, 0)),
            pl.BlockSpec((BLOCK // 2, ocol, cout), lambda i: (i, 0, 0)),
            whole((ocol, mid)),
            whole((ocol, cout)),
            pl.BlockSpec((BLOCK // 2, mid), lambda i: (i, 0)),
            pl.BlockSpec((BLOCK // 2, cout), lambda i: (i, 0)),
            whole((SUB, 128)),
            whole((slots, cout)),
            whole((slots, att)),
            whole((slots, att)),
            whole((slots, 128)),
        ),
        scratch_shapes=[
            pltpu.VMEM((BLOCK, cols + SUB, mid), F32),
            pltpu.VMEM((BLOCK // 2, cols, chan // 2), F32),
            pltpu.VMEM((BLOCK // 2, cols, chan // 2), F32),
            pltpu.VMEM((BLOCK + 1, ocol, 3 * mid), BF16),
            pltpu.VMEM((slots, SUB, cout), F32),
        ],
        compiler_params=params,
        name="forward",
    )(features, up, left, wr, wc, wp, attn_tanh, attn_sigm, ao, live)

    dembed, low, right = pl.pallas_call(
        functools.partial(edge_kernel, sizes, tiles_r, tiles_c),
        out_shape=(
            jax.ShapeDtypeStruct((slots, cout), F32),
            jax.ShapeDtypeStruct((ocol + SUB, mid), F32),
            jax.ShapeDtypeStruct((orow, mid), F32),
        ),
        scratch_shapes=[
            pltpu.VMEM((ocol + orow, mid), BF16),
            pltpu.VMEM((ocol + orow + 2 * SUB, mid), BF16),
            pltpu.SemaphoreType.DMA((3,)),
            pltpu.SemaphoreType.DMA((3,)),
        ]
        + exchange_rooms(sizes),
        compiler_params=pltpu.CompilerParams(collective_id=0, has_side_effects=True),
        name="edge",
    )(pay, embed, tval, gval, score, live, ao, cls, attn_tanh, attn_sigm, wb, row3, row2, col3, col2)

    def turn(i):
        return (steps - 1 - i, 0, 0)

    feature_grad, partial_grad = pl.pallas_call(
        functools.partial(backward_kernel, tiles_c),
        grid=(steps,),
        out_shape=(
            jax.ShapeDtypeStruct((rows, cols, chan), BF16),
            jax.ShapeDtypeStruct((SUB, chan), F32),
        ),
        in_specs=[
            pl.BlockSpec((BLOCK, cols, chan), turn),
            pl.BlockSpec((BLOCK, cols, mid), turn),
            pl.BlockSpec((BLOCK // 2, ocol, mid), turn),
            pl.BlockSpec((BLOCK // 2, ocol, cout), turn),
            whole(dembed.shape),
            pl.BlockSpec((BLOCK // 2, mid), lambda i: (steps - 1 - i, 0)),
            whole(low.shape),
            whole(wb.shape),
            whole(wt.shape),
            whole(wo.shape),
        ],
        out_specs=(pl.BlockSpec((BLOCK, cols, chan), turn), whole((SUB, chan))),
        scratch_shapes=[
            pltpu.VMEM((BLOCK // 2 + 1, ocol + SUB, mid), F32),
            pltpu.VMEM((BLOCK, cols, mid), F32),
            pltpu.VMEM((BLOCK // 2, cols, chan // 2), F32),
            pltpu.VMEM((BLOCK // 2, cols, chan // 2), F32),
        ],
        compiler_params=params,
        name="backward",
    )(features, slope1, slope2, slope3, dembed, right, low, wb, wt, wo)

    new_delta = stain_delta + pl.pallas_call(
        functools.partial(step_kernel, sizes),
        out_shape=jax.ShapeDtypeStruct((1, chan), F32),
        scratch_shapes=exchange_rooms(sizes),
        compiler_params=pltpu.CompilerParams(collective_id=1, has_side_effects=True),
        name="step",
    )(partial_grad, delta, step_dir[None, :])[0]
    return (feature_grad, new_delta)


def solution(mesh):
    return jax.shard_map(
        shards,
        mesh=mesh,
        in_specs=(P("space", "head", None), P(), P("space", "head")) + (P(),) * 9,
        out_specs=(P("space", "head", None), P()),
        check_vma=False,
    )
```

```python
import functools

import jax
import jax.numpy as jnp
from jax import lax
from jax.experimental import pallas as pl
from jax.experimental.pallas import tpu as pltpu
from jax.sharding import PartitionSpec as P

TILE = 64
ALPHA = 1
BLOCK = 32
SUB = 8
F32 = jnp.float32
MESH = pl.DeviceIdType.MESH
BF16 = jnp.bfloat16
HP = lax.Precision.HIGHEST


def sigm(value):
    return 0.5 + 0.5 * jnp.tanh(0.5 * value)


def dot(a, b):
    return jnp.dot(a, b, preferred_element_type=F32)


def column(row, width):
    return jnp.transpose(jnp.broadcast_to(row, (width, row.shape[1])))


def turned(weight):
    return jnp.transpose(weight.astype(F32)).astype(BF16)


def forward_kernel(
    sizes, x_ref, up_ref, left_ref, wr_ref, wc_ref, wp_ref, at_ref, as_ref, ao_ref, cls_ref, wb_ref, tissue_ref,
    slope1_ref, slope2_ref, slope3_ref, dembed_ref, low_ref, right_ref,
    red, lo, hi, taps, sums, row2, row3, col2, col3, *edge_rooms,
):
    step = pl.program_id(0)
    rows, cols, chan = x_ref.shape
    mid = wr_ref.shape[1]
    cout = wp_ref.shape[1]
    orow, ocol = rows // 2, cols // 2
    half = TILE // 2
    tiles_r, tiles_c = tissue_ref.shape

    def put_taps(slot, source):
        for b, start in enumerate((SUB - 1, SUB, SUB + 1)):
            taps[slot, :, b * mid : (b + 1) * mid] = source[pl.ds(start, ocol, stride=2), :].astype(BF16)

    @pl.when(step == 0)
    def _():
        greet(sizes, True)
        put_taps(0, up_ref)
        sums[...] = jnp.zeros_like(sums)

    @pl.when(step > 0)
    def _():
        taps[0] = taps[rows]

    pre = dot(x_ref[...].reshape(rows * cols, chan), wr_ref[...])
    sig = sigm(pre)
    act = pre * sig
    slope1_ref[...] = (sig + act * (1.0 - sig)).reshape(rows, cols, mid).astype(BF16)
    red[:, SUB:, :] = act.reshape(rows, cols, mid)
    for r in range(rows):
        red[r, SUB - 1 : SUB, :] = left_ref[r : r + 1, :]
        put_taps(r + 1, red.at[r])
    acc = jnp.zeros((orow * ocol, mid), F32)
    for a in range(3):
        part = jnp.stack([taps[2 * i + a] for i in range(orow)], axis=0)
        acc = acc + dot(part.reshape(orow * ocol, 3 * mid), wc_ref[a])
    sig = sigm(acc)
    act = acc * sig
    slope2 = (sig + act * (1.0 - sig)).reshape(orow, ocol, mid)
    slope2_ref[...] = slope2.astype(BF16)
    col2[pl.ds(pl.multiple_of(step * orow, orow), orow), :] = slope2[:, 0, :]
    short = []
    for i in range(orow):
        lo[i] = x_ref[2 * i, :, : chan // 2].astype(F32)
        hi[i] = x_ref[2 * i, :, chan // 2 :].astype(F32)
    for i in range(orow):
        short.append(
            jnp.concatenate(
                [lo.at[i][pl.ds(0, ocol, stride=2), :].astype(BF16), hi.at[i][pl.ds(0, ocol, stride=2), :].astype(BF16)],
                axis=1,
            )
        )
    short = jnp.stack(short, axis=0).reshape(orow * ocol, chan)
    preact = dot(jnp.concatenate([act.astype(BF16), short], axis=1), wp_ref[...])
    sig = sigm(preact)
    act = preact * sig
    slope3 = (sig + act * (1.0 - sig)).reshape(orow, ocol, cout)
    slope3_ref[...] = slope3.astype(BF16)
    col3[pl.ds(pl.multiple_of(step * orow, orow), orow), :] = slope3[:, 0, :]

    @pl.when(step == 0)
    def _():
        row2[...] = slope2_ref[0]
        row3[...] = slope3_ref[0]

    cells = jnp.sum(act.reshape(orow, tiles_c, half // SUB, SUB, cout), axis=(0, 2))
    trow = (step * orow) // half
    for c in range(tiles_c):
        slot = trow * tiles_c + c
        sums[slot] = sums[slot] + cells[c]

    @pl.when(step == pl.num_programs(0) - 1)
    def _():
        finish(
            sizes, tiles_r, tiles_c, sums, at_ref, as_ref, ao_ref, cls_ref, wb_ref, tissue_ref, row2, row3, col2, col3,
            dembed_ref, low_ref, right_ref, *edge_rooms,
        )


AXES = ("head", "space")


def peer(sizes, k, hop):
    place = tuple(lax.axis_index(axis) for axis in AXES)
    other = lax.rem(place[k] + hop, sizes[k])
    return (other, place[1]) if k == 0 else (place[0], other)


def corner_of(sizes, hop):
    return tuple(lax.rem(lax.axis_index(axis) + n + hop, n) for axis, n in zip(AXES, sizes))


def greet(sizes, corners):
    barrier = pltpu.get_barrier_semaphore()
    for k in range(2):
        for hop in range(1, sizes[k]):
            pl.semaphore_signal(barrier, inc=1, device_id=peer(sizes, k, hop), device_id_type=MESH)
    if corners:
        for hop in (-1, 1):
            pl.semaphore_signal(barrier, inc=1, device_id=corner_of(sizes, hop), device_id_type=MESH)


def wait_greetings(sizes, corners):
    pl.semaphore_wait(pltpu.get_barrier_semaphore(), sizes[0] + sizes[1] - 2 + (2 if corners else 0))


def exchanged(sizes, first, combine, rooms):
    got0, got1, mine, send0, send1, recv0, recv1 = rooms
    mine[0] = first
    for k in range(2):
        got, send, recv = (got0, got1)[k], (send0, send1)[k], (recv0, recv1)[k]
        copies = [
            pltpu.make_async_remote_copy(
                src_ref=mine.at[k],
                dst_ref=got.at[hop],
                send_sem=send.at[hop],
                recv_sem=recv.at[hop],
                device_id=peer(sizes, k, hop),
                device_id_type=MESH,
            )
            for hop in range(1, sizes[k])
        ]
        for copy in copies:
            copy.start()
        got[0] = mine[k]
        for copy in copies:
            copy.wait()
        result = combine(got[...])
        if k == 0:
            mine[1] = result
    return result


def exchange_rooms(sizes):
    shape = (SUB, 128)
    return [
        pltpu.VMEM((sizes[0],) + shape, F32),
        pltpu.VMEM((sizes[1],) + shape, F32),
        pltpu.VMEM((2,) + shape, F32),
        pltpu.SemaphoreType.DMA((sizes[0],)),
        pltpu.SemaphoreType.DMA((sizes[1],)),
        pltpu.SemaphoreType.DMA((sizes[0],)),
        pltpu.SemaphoreType.DMA((sizes[1],)),
    ]


def rim_kernel(
    sizes, row_ref, col_ref, delta_ref, wr_ref, ws_ref, we_ref, sp_ref,
    up_out, left_out, wr_out, wp_out, wb_out, wt_out, wo_out,
    edges, landed, edge_send, edge_recv,
):
    targets = (peer(sizes, 1, 1), peer(sizes, 0, 1), corner_of(sizes, 1))
    sources = (peer(sizes, 1, sizes[1] - 1), peer(sizes, 0, sizes[0] - 1), corner_of(sizes, -1))
    barrier = pltpu.get_barrier_semaphore()
    for device in targets + sources:
        pl.semaphore_signal(barrier, inc=1, device_id=device, device_id_type=MESH)
    mid, cout = we_ref.shape
    cols, rows = row_ref.shape[1], col_ref.shape[0]
    wide = column(1.0 + delta_ref[...], mid)
    wr = wr_ref[...].astype(F32) * wide
    wr_out[...] = wr.astype(BF16)
    col = col_ref[:, SUB:, :].astype(F32)[:, SUB - 1, :].astype(BF16)
    both = dot(jnp.concatenate([row_ref[0], col], axis=0), wr.astype(BF16))
    edges[...] = (both * sigm(both)).astype(BF16)
    spans = ((0, cols, 0), (cols, rows, cols), (cols - 2 * SUB, 2 * SUB, cols + rows))
    copies = [
        pltpu.make_async_remote_copy(
            src_ref=edges.at[pl.ds(source, size)],
            dst_ref=landed.at[pl.ds(place, size)],
            send_sem=edge_send.at[k],
            recv_sem=edge_recv.at[k],
            device_id=targets[k],
            device_id_type=MESH,
        )
        for k, (source, size, place) in enumerate(spans)
    ]
    pl.semaphore_wait(barrier, 6)
    for copy in copies:
        copy.start()
    wo_out[...] = turned(wr)
    wp_out[:mid, :] = we_ref[...]
    wb_out[:, :mid] = turned(we_ref[...])
    for k in range(cout // mid):
        at = slice(k * mid, (k + 1) * mid)
        ws = ws_ref[:, at].astype(F32) * wide
        wp_out[mid:, at] = ws.astype(BF16)
        wb_out[at, mid:] = turned(ws)
    taps = (
        ((1, 1), (1, 2), (2, 1), (2, 2)),
        (None, (1, 0), None, (2, 0)),
        (None, None, (0, 1), (0, 2)),
        (None, None, None, (0, 0)),
    )
    for i, line in enumerate(taps):
        for j, tap in enumerate(line):
            value = jnp.zeros((mid, mid), BF16) if tap is None else turned(sp_ref[tap[0], tap[1]])
            wt_out[i * mid : (i + 1) * mid, j * mid : (j + 1) * mid] = value
    for copy in copies:
        copy.wait()
    above = jnp.where(lax.axis_index("space") > 0, 1.0, 0.0)
    beside = jnp.where(lax.axis_index("head") > 0, 1.0, 0.0)
    up_out[0:SUB, :] = landed[cols + rows :, :].astype(F32)[SUB:] * (above * beside)
    up_out[SUB:, :] = landed[0:cols, :].astype(F32) * above
    left_out[...] = landed[cols : cols + rows, :].astype(F32) * beside


def step_kernel(sizes, grad_ref, delta_ref, dir_ref, out_ref, *rooms):
    greet(sizes, False)
    wait_greetings(sizes, False)
    chan = grad_ref.shape[1]
    lines = chan // 128
    part = jnp.sum(grad_ref[...], axis=0, keepdims=True)
    part = [part[:, k * 128 : (k + 1) * 128] for k in range(lines)]
    part = jnp.concatenate(part + [jnp.zeros((SUB - lines, 128), F32)], axis=0)
    total = exchanged(sizes, part, lambda every: jnp.sum(every, axis=0), rooms)
    delta = delta_ref[...]
    ddelta = jnp.concatenate([total[k : k + 1] for k in range(lines)], axis=1) / (1.0 + delta)
    norm = jnp.sqrt(jnp.sum(ddelta * ddelta, axis=1, keepdims=True) * (1.0 / chan) + 1e-06)
    out_ref[...] = (2 * dir_ref[...] - 1).astype(F32) * float(ALPHA) * ddelta / norm


def spread(dembed_ref, first, tiles_c, half):
    cout = dembed_ref.shape[1]
    return jnp.concatenate(
        [jnp.broadcast_to(dembed_ref[pl.ds(first + c, 1), :], (half, cout)) for c in range(tiles_c)], axis=0
    )


def finish(
    sizes, tiles_r, tiles_c, sums, at_ref, as_ref, ao_ref, cls_ref, wb_ref, tissue_ref, row2, row3, col2, col3,
    dembed_ref, low_ref, right_ref, edges, landed, edge_send, edge_recv, *rooms,
):
    half = TILE // 2
    cout = cls_ref.shape[1]
    lines = cout // 128
    ao, cls = ao_ref[...], cls_ref[...]
    embed = jnp.sum(sums[...], axis=1) * (1.0 / (half * half))
    tval = jnp.tanh(jnp.dot(embed, at_ref[...], precision=HP, preferred_element_type=F32))
    gval = sigm(jnp.dot(embed, as_ref[...], precision=HP, preferred_element_type=F32))
    score = jnp.sum(tval * gval * ao, axis=1, keepdims=True)
    slot = lax.broadcasted_iota(jnp.int32, (embed.shape[0], 128), 0)
    marks = jnp.zeros(slot.shape, jnp.int32)
    for r in range(tiles_r):
        for c in range(tiles_c):
            mark = jnp.broadcast_to(tissue_ref[r : r + 1, c : c + 1], slot.shape)
            marks = jnp.where(slot == r * tiles_c + c, mark, marks)
    live = marks[:, 0:1] > 0
    top = jnp.max(jnp.where(live, score, -1e30), axis=0, keepdims=True)
    weight = jnp.where(live, jnp.exp(score - top), 0.0)
    vector = jnp.sum(weight * embed, axis=0, keepdims=True)
    payload = jnp.concatenate(
        [vector[:, k * 128 : (k + 1) * 128] for k in range(lines)]
        + [
            jnp.broadcast_to(jnp.sum(weight, axis=0, keepdims=True), (1, 128)),
            jnp.broadcast_to(top, (1, 128)),
            jnp.zeros((SUB - lines - 2, 128), F32),
        ],
        axis=0,
    )

    def combine(every):
        top = jnp.max(every[:, lines + 1 : lines + 2, :], axis=0)
        factor = jnp.exp(every[:, lines + 1 : lines + 2, :] - top[None])
        total = jnp.sum(every[:, : lines + 1, :] * factor, axis=0)
        return jnp.concatenate([total, top, jnp.zeros((SUB - lines - 2, 128), F32)], axis=0)

    wait_greetings(sizes, True)
    comb = exchanged(sizes, payload, combine, rooms)
    total, top = comb[lines : lines + 1, 0:1], comb[lines + 1 : lines + 2, 0:1]
    pooled = jnp.concatenate([comb[k : k + 1] for k in range(lines)], axis=1) / total
    prob = jnp.where(live, jnp.exp(score - top), 0.0) / total
    gap = jnp.sum(embed * cls, axis=1, keepdims=True) - jnp.sum(pooled * cls, axis=1, keepdims=True)
    datt = (prob * gap) * ao
    dtanh = datt * gval * (1.0 - tval * tval)
    dsigm = datt * tval * gval * (1.0 - gval)
    back = (((1,), (1,)), ((), ()))
    dembed = (
        prob * cls
        + lax.dot_general(dtanh, at_ref[...], back, precision=HP, preferred_element_type=F32)
        + lax.dot_general(dsigm, as_ref[...], back, precision=HP, preferred_element_type=F32)
    ) * (1.0 / (half * half))
    dembed_ref[...] = dembed
    ocol, mid = row2.shape
    orow = col2.shape[0]
    we = wb_ref[:, :mid]

    def spread_rows(rows):
        return jnp.concatenate([jnp.broadcast_to(dembed[t : t + 1], (half, cout)) for t in rows], axis=0)

    dpre = (row3[...].astype(F32) * spread_rows(range(tiles_c))).astype(BF16)
    edges[0:ocol, :] = (dot(dpre, we) * row2[...].astype(F32)).astype(BF16)
    dpre = (col3[...] * spread_rows(range(0, tiles_r * tiles_c, tiles_c))).astype(BF16)
    edges[ocol : ocol + orow, :] = (dot(dpre, we) * col2[...]).astype(BF16)
    spans = ((0, ocol, 0), (ocol, orow, ocol), (0, 2 * SUB, ocol + orow))
    targets = (peer(sizes, 1, sizes[1] - 1), peer(sizes, 0, sizes[0] - 1), corner_of(sizes, -1))
    copies = [
        pltpu.make_async_remote_copy(
            src_ref=edges.at[pl.ds(source, size)],
            dst_ref=landed.at[pl.ds(place, size)],
            send_sem=edge_send.at[k],
            recv_sem=edge_recv.at[k],
            device_id=targets[k],
            device_id_type=MESH,
        )
        for k, (source, size, place) in enumerate(spans)
    ]
    for copy in copies:
        copy.start()
    for copy in copies:
        copy.wait()
    inner = [lax.axis_index(axis) < n - 1 for axis, n in zip(AXES, sizes)]
    below = jnp.where(inner[1], 1.0, 0.0)
    beside = jnp.where(inner[0], 1.0, 0.0)
    low_ref[0:ocol, :] = landed[0:ocol, :].astype(F32) * below
    right_ref[...] = landed[ocol : ocol + orow, :].astype(F32) * beside
    low_ref[ocol:, :] = landed[ocol + orow :, :].astype(F32)[:SUB] * (below * beside)


def backward_kernel(
    tiles_c, x_ref, slope1_ref, slope2_ref, slope3_ref, dembed_ref, right_ref, low_ref, wb_ref, wt_ref, wo_ref,
    out_ref, grad_ref, dsx, drs, slo, shi,
):
    step = pl.program_id(0)
    rows, cols, chan = x_ref.shape
    orow, ocol, mid = slope2_ref.shape
    cout = slope3_ref.shape[2]
    half = TILE // 2
    block = pl.num_programs(0) - 1 - step
    trow = (block * orow) // half

    @pl.when(step == 0)
    def _():
        dsx[orow, :, :] = low_ref[...]
        slo[...] = jnp.zeros_like(slo)
        shi[...] = jnp.zeros_like(shi)
        grad_ref[...] = jnp.zeros_like(grad_ref)

    @pl.when(step > 0)
    def _():
        dsx[orow] = dsx[0]

    dpre = (slope3_ref[...].astype(F32) * spread(dembed_ref, trow * tiles_c, tiles_c, half)[None]).astype(BF16)
    both = dot(dpre.reshape(orow * ocol, cout), wb_ref[...])
    dsx[0:orow, 0:ocol, :] = both[:, :mid].reshape(orow, ocol, mid) * slope2_ref[...].astype(F32)
    for i in range(orow):
        dsx[i, ocol : ocol + 1, :] = right_ref[i : i + 1, :]
        slo[i, pl.ds(0, ocol, stride=2), :] = both[i * ocol : (i + 1) * ocol, mid : mid + chan // 2]
        shi[i, pl.ds(0, ocol, stride=2), :] = both[i * ocol : (i + 1) * ocol, mid + chan // 2 :]
    four = jnp.concatenate(
        [
            dsx[di : di + orow, dj : dj + ocol, :].astype(BF16).reshape(orow * ocol, mid)
            for di in range(2)
            for dj in range(2)
        ],
        axis=1,
    )
    grads = dot(four, wt_ref[...])
    for i in range(orow):
        for di in range(2):
            for dj in range(2):
                n = 2 * di + dj
                drs[2 * i + di, pl.ds(dj, ocol, stride=2), :] = grads[i * ocol : (i + 1) * ocol, n * mid : (n + 1) * mid]
    dred = (drs[...] * slope1_ref[...].astype(F32)).astype(BF16)
    dinput = dot(dred.reshape(rows * cols, mid), wo_ref[...]).reshape(rows, cols, chan)
    total = jnp.zeros((SUB, chan), F32)
    for r in range(rows):
        value = dinput[r]
        if r % 2 == 0:
            value = value + jnp.concatenate([slo[r // 2], shi[r // 2]], axis=1)
        out_ref[r] = value.astype(BF16)
        total = total + jnp.sum((value * x_ref[r].astype(F32)).reshape(cols // SUB, SUB, chan), axis=0)
    grad_ref[...] += total


def whole(shape):
    return pl.BlockSpec(shape, lambda i: (0,) * len(shape))


def shards(
    features,
    stain_delta,
    tissue,
    reduce_weight,
    spatial_weight,
    expand_weight,
    shortcut_weight,
    attn_tanh,
    attn_sigm,
    attn_out,
    classifier,
    step_dir,
):
    rows, cols, chan = features.shape
    mid = reduce_weight.shape[1]
    cout = expand_weight.shape[1]
    att = attn_out.shape[0]
    tiles_r, tiles_c = tissue.shape
    slots = -(-tiles_r * tiles_c // SUB) * SUB
    orow, ocol = rows // 2, cols // 2
    delta = stain_delta[None, :]
    wc = spatial_weight.reshape(3, 3 * mid, mid)
    ao = attn_out[None, :]
    cls = classifier[None, :]
    sizes = tuple(lax.axis_size(axis) for axis in AXES)

    up, left, wr, wp, wb, wt, wo = pl.pallas_call(
        functools.partial(rim_kernel, sizes),
        grid=(1,),
        out_shape=(
            jax.ShapeDtypeStruct((cols + SUB, mid), F32),
            jax.ShapeDtypeStruct((rows, mid), F32),
            jax.ShapeDtypeStruct((chan, mid), BF16),
            jax.ShapeDtypeStruct((mid + chan, cout), BF16),
            jax.ShapeDtypeStruct((cout, mid + chan), BF16),
            jax.ShapeDtypeStruct((4 * mid, 4 * mid), BF16),
            jax.ShapeDtypeStruct((mid, chan), BF16),
        ),
        in_specs=[
            pl.BlockSpec((1, cols, chan), lambda i: (rows - 1, 0, 0)),
            pl.BlockSpec((rows, 2 * SUB, chan), lambda i: (0, cols // (2 * SUB) - 1, 0)),
            whole(delta.shape),
            whole(reduce_weight.shape),
            whole(shortcut_weight.shape),
            whole(expand_weight.shape),
            whole(spatial_weight.shape),
        ],
        out_specs=(
            whole((cols + SUB, mid)),
            whole((rows, mid)),
            whole((chan, mid)),
            whole((mid + chan, cout)),
            whole((cout, mid + chan)),
            whole((4 * mid, 4 * mid)),
            whole((mid, chan)),
        ),
        scratch_shapes=[
            pltpu.VMEM((cols + rows, mid), BF16),
            pltpu.VMEM((cols + rows + 2 * SUB, mid), BF16),
            pltpu.SemaphoreType.DMA((3,)),
            pltpu.SemaphoreType.DMA((3,)),
        ],
        compiler_params=pltpu.CompilerParams(collective_id=2, has_side_effects=True),
        name="rim",
    )(features, features, delta, reduce_weight, shortcut_weight, expand_weight, spatial_weight)

    steps = rows // BLOCK
    params = pltpu.CompilerParams(dimension_semantics=("arbitrary",), vmem_limit_bytes=56 * 1024 * 1024)
    slope1, slope2, slope3, dembed, low, right = pl.pallas_call(
        functools.partial(forward_kernel, sizes),
        grid=(steps,),
        out_shape=(
            jax.ShapeDtypeStruct((rows, cols, mid), BF16),
            jax.ShapeDtypeStruct((orow, ocol, mid), BF16),
            jax.ShapeDtypeStruct((orow, ocol, cout), BF16),
            jax.ShapeDtypeStruct((slots, cout), F32),
            jax.ShapeDtypeStruct((ocol + SUB, mid), F32),
            jax.ShapeDtypeStruct((orow, mid), F32),
        ),
        in_specs=[
            pl.BlockSpec((BLOCK, cols, chan), lambda i: (i, 0, 0)),
            whole(up.shape),
            pl.BlockSpec((BLOCK, mid), lambda i: (i, 0)),
            whole(wr.shape),
            whole(wc.shape),
            whole(wp.shape),
            whole(attn_tanh.shape),
            whole(attn_sigm.shape),
            whole(ao.shape),
            whole(cls.shape),
            whole(wb.shape),
            whole(tissue.shape),
        ],
        out_specs=(
            pl.BlockSpec((BLOCK, cols, mid), lambda i: (i, 0, 0)),
            pl.BlockSpec((BLOCK // 2, ocol, mid), lambda i: (i, 0, 0)),
            pl.BlockSpec((BLOCK // 2, ocol, cout), lambda i: (i, 0, 0)),
            whole((slots, cout)),
            whole((ocol + SUB, mid)),
            whole((orow, mid)),
        ),
        scratch_shapes=[
            pltpu.VMEM((BLOCK, cols + SUB, mid), F32),
            pltpu.VMEM((BLOCK // 2, cols, chan // 2), F32),
            pltpu.VMEM((BLOCK // 2, cols, chan // 2), F32),
            pltpu.VMEM((BLOCK + 1, ocol, 3 * mid), BF16),
            pltpu.VMEM((slots, SUB, cout), F32),
            pltpu.VMEM((ocol, mid), BF16),
            pltpu.VMEM((ocol, cout), BF16),
            pltpu.VMEM((orow, mid), F32),
            pltpu.VMEM((orow, cout), F32),
            pltpu.VMEM((ocol + orow, mid), BF16),
            pltpu.VMEM((ocol + orow + 2 * SUB, mid), BF16),
            pltpu.SemaphoreType.DMA((3,)),
            pltpu.SemaphoreType.DMA((3,)),
        ]
        + exchange_rooms(sizes),
        compiler_params=pltpu.CompilerParams(
            dimension_semantics=("arbitrary",),
            vmem_limit_bytes=56 * 1024 * 1024,
            collective_id=0,
            has_side_effects=True,
        ),
        name="forward",
    )(features, up, left, wr, wc, wp, attn_tanh, attn_sigm, ao, cls, wb, tissue)

    def turn(i):
        return (steps - 1 - i, 0, 0)

    feature_grad, partial_grad = pl.pallas_call(
        functools.partial(backward_kernel, tiles_c),
        grid=(steps,),
        out_shape=(
            jax.ShapeDtypeStruct((rows, cols, chan), BF16),
            jax.ShapeDtypeStruct((SUB, chan), F32),
        ),
        in_specs=[
            pl.BlockSpec((BLOCK, cols, chan), turn),
            pl.BlockSpec((BLOCK, cols, mid), turn),
            pl.BlockSpec((BLOCK // 2, ocol, mid), turn),
            pl.BlockSpec((BLOCK // 2, ocol, cout), turn),
            whole(dembed.shape),
            pl.BlockSpec((BLOCK // 2, mid), lambda i: (steps - 1 - i, 0)),
            whole(low.shape),
            whole(wb.shape),
            whole(wt.shape),
            whole(wo.shape),
        ],
        out_specs=(pl.BlockSpec((BLOCK, cols, chan), turn), whole((SUB, chan))),
        scratch_shapes=[
            pltpu.VMEM((BLOCK // 2 + 1, ocol + SUB, mid), F32),
            pltpu.VMEM((BLOCK, cols, mid), F32),
            pltpu.VMEM((BLOCK // 2, cols, chan // 2), F32),
            pltpu.VMEM((BLOCK // 2, cols, chan // 2), F32),
        ],
        compiler_params=params,
        name="backward",
    )(features, slope1, slope2, slope3, dembed, right, low, wb, wt, wo)

    new_delta = stain_delta + pl.pallas_call(
        functools.partial(step_kernel, sizes),
        out_shape=jax.ShapeDtypeStruct((1, chan), F32),
        scratch_shapes=exchange_rooms(sizes),
        compiler_params=pltpu.CompilerParams(collective_id=1, has_side_effects=True),
        name="step",
    )(partial_grad, delta, step_dir[None, :])[0]
    return (feature_grad, new_delta)


def solution(mesh):
    return jax.shard_map(
        shards,
        mesh=mesh,
        in_specs=(P("space", "head", None), P(), P("space", "head")) + (P(),) * 9,
        out_specs=(P("space", "head", None), P()),
        check_vma=False,
    )
```
